256 devices in a mesh: group: 2 (over y_hi), fsdp: 128 (over y_lo, z, x, core).
Axes of the slice: x: 4, y: 4 (y_hi: 2, y_lo: 2; y = y_hi * 2 + y_lo), z: 8, core: 2. Of those that a mesh axis runs over, the one named last changes fastest.
Arguments:
- teacher_rows: bfloat16 [163840, 2048], P(('group', 'fsdp')), may hold values from -6 to 6
- student_rows: bfloat16 [163840, 1024], P(('group', 'fsdp')), may hold values from -24 to 24
- counts: int32 [256], P(('group', 'fsdp')), may hold values from 213 to 640, as said below
- teacher_weight: bfloat16 [2048, 4096], P(None, ('group', 'fsdp')), may hold values from -0.125 to 0.125
- teacher_bias: float32 [4096], replicated, may hold values from -6 to 6
- teacher_gain: float32 [4096], replicated, may hold values from 0.1 to 1.9
- teacher_head: float32 [4096], replicated, may hold values from -0.09375 to 0.09375
- cross_weight: bfloat16 [1024, 1024], replicated, may hold values from -0.1875 to 0.1875
- cross_bias: float32 [1024], replicated, may hold values from -3 to 3
- out_weight: float32 [1024], replicated, may hold values from -0.1875 to 0.1875
Outputs:
- grad_cross: float32 [1024, 1024], P('fsdp')
- grad_bias: float32 [1024], replicated
- grad_out: float32 [1024], replicated
The draws below stay inside these ranges and needn't reach their ends.
Inputs may be any that keep to these rules, and one draw needn't show every extreme that they name: counts[i] live impressions fill the first slots of shard i, the rest of its 640 slots are padding.
All inputs are finite; a program needn't handle non-finite values.
Results may differ from the reference program's by a relative error of at most 0.00035.
The reference program's roundings to bfloat16 on the way (of `dcross_half`) count: a program that leaves them out, or rounds other values in their place, can miss the bound.
Values may be sent and summed in bfloat16 or wider, within the bound.
No kernel may reach another device: no remote copies, remote signals or barrier semaphores. Data moves between devices by JAX's collectives and lax.ppermute only.
A program may use at most 128 MiB of HBM per device.

```python
import math
import jax
import jax.numpy as jnp
from jax import lax

FIN = 2048
DT = 4096
DS = 1024
ROWS_DEV = 640
SHARDS = 256
IMPR = 163840
N_GROUP = 2
N_FSDP = 128


def draw_counts(key, part):
    lowest = ROWS_DEV // 3
    spread = max(ROWS_DEV // 8, 1)
    position = jnp.arange(SHARDS, dtype=jnp.int32)
    trend = lowest + (ROWS_DEV - lowest) * position // max(SHARDS - 1, 1)
    jitter = jax.random.randint(key, (SHARDS,), -spread, spread + 1, dtype=jnp.int32)
    values = jnp.clip(trend + jitter, lowest, ROWS_DEV)
    values = values.at[0].set(lowest)
    values = values.at[SHARDS - 1].set(ROWS_DEV)
    return values.astype(jnp.int32)


def strengthened(array, stream_key, source, target, parts, factor):
    owner, partner = [(jnp.arange(array.shape[dim]) // (array.shape[dim] // parts)).reshape([-1 if axis == dim else 1 for axis in range(array.ndim)]) for dim in (source, target)]
    chosen = jax.random.permutation(stream_key, parts)[partner]
    strong = (owner == chosen) | (owner == (partner + parts // 2) % parts)
    return jnp.where(strong, factor * array, array)


def shard_levels(stream_key, extent, shards, smallest, largest):
    def one(axis_at, shards_of):
        steps = jax.random.uniform(jax.random.fold_in(jax.random.fold_in(stream_key, 6), axis_at), (shards_of,), jnp.float32, smallest / len(shards), largest / len(shards))
        return jnp.repeat(jnp.exp(steps), extent[axis_at] // shards_of).reshape((-1,) + (1,) * (len(extent) - axis_at - 1))

    level = one(*shards[0])
    for cut in shards[1:]:
        level = level * one(*cut)
    return level


def gaussian(stream_key, dims, deviation, most, split=(), held_as=jnp.bfloat16):
    values = jax.random.normal(stream_key, dims, jnp.float32) * deviation
    if len(split) > 0:
        values = shard_levels(stream_key, dims, split, -0.22, 0.18) * values
    return jnp.clip(values, min=-most, max=most).astype(held_as)


def heavy_noise(rng, extent, width, reach, cuts, heavy, kind=jnp.bfloat16):
    result = width * jax.random.normal(rng, extent, jnp.float32)
    if cuts:
        result = result * shard_levels(rng, extent, cuts, -0.22, 0.18)
    return jnp.clip(strengthened(result, jax.random.fold_in(rng, 3), *heavy), -reach, reach).astype(kind)


def setup_inputs(seed: int = 0) -> dict:
    keys = jax.random.split(jax.random.key(seed), 11)
    return {
        "teacher_rows": gaussian(keys[0], (IMPR, FIN), 1.0, 6.0, ((0, 256),)),
        "student_rows": heavy_noise(keys[1], (IMPR, DS), 1.0, 24.0, ((0, 256),), (0, 1, 256, 6.0)),
        "counts": draw_counts(jax.random.fold_in(keys[10], 71), 0),
        "teacher_weight": gaussian(keys[3], (FIN, DT), FIN ** -0.5, 0.125, ((1, 256),)),
        "teacher_bias": gaussian(keys[4], (DT,), 1.0, 6.0, (), jnp.float32),
        "teacher_gain": jnp.clip(1.0 + 0.18 * jax.random.normal(keys[5], (DT,), jnp.float32), 0.1, 1.9),
        "teacher_head": gaussian(keys[6], (DT,), DT ** -0.5, 0.09375, (), jnp.float32),
        "cross_weight": gaussian(keys[7], (DS, DS), DS ** -0.5, 0.1875),
        "cross_bias": gaussian(keys[8], (DS,), 0.5, 3.0, (), jnp.float32),
        "out_weight": gaussian(keys[9], (DS,), DS ** -0.5, 0.1875, (), jnp.float32),
    }


epsilon = 1e-06

def local_terms(rows_t, rows_s, amount, teacher_weight, teacher_bias, teacher_gain, teacher_head, cross_weight, cross_bias, out_weight, loss_scale):
    preact = jnp.dot(rows_t, teacher_weight, preferred_element_type=jnp.float32) + teacher_bias
    meansq = lax.optimization_barrier(jnp.mean(preact * preact, axis=-1, keepdims=True))
    normed = preact * lax.rsqrt(meansq + epsilon) * teacher_gain
    teacher_logit = lax.optimization_barrier(jnp.sum(jax.nn.silu(normed) * teacher_head, axis=-1))
    cross = jnp.dot(rows_s, cross_weight, preferred_element_type=jnp.float32) + cross_bias
    inputs_f = rows_s.astype(jnp.float32)
    mixed = inputs_f * cross + inputs_f
    student_logit = lax.optimization_barrier(jnp.sum(mixed * out_weight, axis=-1))
    live_rows = (jnp.arange(rows_t.shape[0], dtype=jnp.int32) < amount).astype(jnp.float32)
    error = (student_logit - teacher_logit) * live_rows * loss_scale
    dcross = error[:, None] * out_weight[None, :] * inputs_f
    dcross_half = dcross.astype(jnp.bfloat16)
    term_w = lax.dot_general(rows_s, dcross_half, (((0,), (0,)), ((), ())), preferred_element_type=jnp.float32)
    term_b = lax.optimization_barrier(jnp.sum(dcross, axis=0))
    term_o = lax.optimization_barrier(jnp.sum(error[:, None] * mixed, axis=0))
    return (term_w, term_b, term_o)

def reference(teacher_rows, student_rows, counts, teacher_weight, teacher_bias, teacher_gain, teacher_head, cross_weight, cross_bias, out_weight):
    shard_count = N_GROUP * N_FSDP
    loss_scale = math.sqrt(DS / (ROWS_DEV * shard_count))
    blocks_t = teacher_rows.reshape(shard_count, ROWS_DEV, FIN)
    blocks_s = student_rows.reshape(shard_count, ROWS_DEV, DS)

    def visit(carry, inputs):
        rows_t, rows_s, amount = inputs
        terms = local_terms(rows_t, rows_s, amount, teacher_weight, teacher_bias, teacher_gain, teacher_head, cross_weight, cross_bias, out_weight, loss_scale)
        return ((carry[0] + terms[0], carry[1] + terms[1], carry[2] + terms[2]), None)
    start_sums = (jnp.zeros((DS, DS), jnp.float32), jnp.zeros((DS,), jnp.float32), jnp.zeros((DS,), jnp.float32))
    totals, unused = lax.scan(visit, start_sums, (blocks_t, blocks_s, counts))
    return (totals[0], totals[1], totals[2])
```

```python
import math

import jax
import jax.numpy as jnp
from jax import lax
from jax.sharding import Mesh
from jax.sharding import PartitionSpec as P

FSDP = ("fsdp_0", "fsdp_1", "fsdp_2", "fsdp_3")
GROUP_FSDP = ("group", "fsdp_0", "fsdp_1", "fsdp_2", "fsdp_3")
SIZES = (4, 8, 4, 2)


epsilon = 1e-06


def ring_pairs(dims, step):
    ny, nz, nx, nc = SIZES
    pairs = []
    for y in range(ny):
        for z in range(nz):
            for x in range(nx):
                for c in range(nc):
                    to = [y, z, x, c]
                    to[dims[c]] = (to[dims[c]] + step) % SIZES[dims[c]]
                    pairs.append((flat(y, z, x, c), flat(*to)))
    return pairs


def flat(y, z, x, c):
    return ((y * SIZES[1] + z) * SIZES[2] + x) * SIZES[3] + c


def ring_gather(block, dims):
    half = block.shape[0] // 2
    plus, minus = ring_pairs(dims, 1), ring_pairs(dims, -1)
    left = lax.ppermute(block, GROUP_FSDP, plus)
    right = lax.ppermute(block, GROUP_FSDP, minus)
    first = lax.ppermute(left[:half], GROUP_FSDP, plus)
    second = lax.ppermute(right[half:], GROUP_FSDP, minus)
    return block, left, right, first, second


def ring_order(array, axis, start):
    turned = lax.dynamic_slice_in_dim(
        jnp.concatenate([array, array], axis=axis), start, 4, axis=axis
    )
    parts = [lax.slice_in_dim(turned, i, i + 1, axis=axis) for i in (0, 3, 1, 2)]
    return jnp.concatenate(parts, axis=axis)


def swap_cores(value):
    return lax.ppermute(value, "fsdp_3", ((0, 1), (1, 0)))


def shards(
    teacher_rows,
    student_rows,
    counts,
    teacher_weight,
    teacher_bias,
    teacher_gain,
    teacher_head,
    cross_weight,
    cross_bias,
    out_weight,
):
    rows = teacher_rows.shape[0]
    width_t = teacher_bias.shape[0]
    width_s = cross_weight.shape[0]
    half_s = width_s // 2
    local = teacher_weight.shape[1]
    loss_scale = math.sqrt(width_s / (rows * lax.axis_size(GROUP_FSDP)))
    y_at, x_at, core = lax.axis_index(("group", "fsdp_0")), lax.axis_index("fsdp_2"), lax.axis_index("fsdp_3")
    group = lax.axis_index("group")

    t_rows = (teacher_rows, swap_cores(teacher_rows))
    s_rows = (student_rows, swap_cores(student_rows))

    mine = teacher_weight.T
    along_z = lax.all_to_all(
        jnp.broadcast_to(mine[None], (8, *mine.shape)), "fsdp_1", 0, 0, tiled=True
    ).reshape(8 * local, -1)
    plane = jnp.concatenate(ring_gather(along_z, (2, 0)), axis=0)
    blocks = ring_gather(plane, (0, 2))

    vectors = jnp.stack([teacher_bias, teacher_gain, teacher_head]).reshape(3, 4, 8, 4, 2, local)
    vectors = lax.dynamic_index_in_dim(vectors, core, 4, keepdims=False)
    vectors = jnp.where(
        core == 0, vectors.transpose(0, 1, 3, 2, 4), vectors.transpose(0, 3, 1, 2, 4)
    )
    vectors = ring_order(vectors, 1, jnp.where(core == 0, y_at, x_at))
    vectors = ring_order(vectors, 2, jnp.where(core == 0, x_at, y_at))
    bias, gain, head = vectors.reshape(3, width_t // 2)

    cut = core * half_s
    cross_half = lax.dynamic_slice_in_dim(cross_weight, cut, half_s, axis=1)
    cross_bias_half = lax.dynamic_slice_in_dim(cross_bias, cut, half_s)
    out_half = lax.dynamic_slice_in_dim(out_weight, cut, half_s)
    inputs, mixed, student_part = [], [], []
    for r in s_rows:
        cross = jnp.dot(r, cross_half, preferred_element_type=jnp.float32) + cross_bias_half
        x = lax.dynamic_slice_in_dim(r, cut, half_s, axis=1).astype(jnp.float32)
        m = x * cross + x
        inputs.append(x)
        mixed.append(m)
        student_part.append(jnp.sum(m * out_half, axis=-1))

    preact = [[], []]
    squares = [0.0, 0.0]
    at = 0
    starts = []
    for block in blocks:
        size = block.shape[0]
        for i, r in enumerate(t_rows):
            p = lax.dot_general(
                r, block, (((1,), (1,)), ((), ())), preferred_element_type=jnp.float32
            ) + bias[at : at + size]
            preact[i].append(p)
            squares[i] = squares[i] + jnp.sum(p * p, axis=-1)
        starts.append((at, size))
        at += size

    lane = jnp.concatenate(
        [squares[0], squares[1], jnp.broadcast_to(counts.astype(jnp.float32), (128,))]
    )
    other = swap_cores(lane)
    squares = (squares[0] + other[rows : 2 * rows], squares[1] + other[:rows])
    amounts = (counts[0].astype(jnp.float32), other[2 * rows])

    part = []
    for i in range(2):
        scale = lax.rsqrt(squares[i][:, None] / width_t + epsilon)
        logit = 0.0
        for (start, size), p in zip(starts, preact[i]):
            normed = p * scale * gain[start : start + size]
            gated = 0.5 * normed * (1.0 + jnp.tanh(0.5 * normed))
            logit = logit + jnp.sum(gated * head[start : start + size], axis=-1)
        part.append(student_part[i] - logit)
    part = jnp.concatenate(part)
    other = swap_cores(part)
    place = jnp.arange(rows, dtype=jnp.int32).astype(jnp.float32)
    term_w, term_b, term_o = 0.0, 0.0, 0.0
    for i in range(2):
        differ = part[i * rows : (i + 1) * rows] + other[(1 - i) * rows : (2 - i) * rows]
        error = differ * (place < amounts[i]).astype(jnp.float32) * loss_scale
        dcross = error[:, None] * out_half[None, :] * inputs[i]
        term_b = term_b + jnp.sum(dcross, axis=0)
        term_o = term_o + jnp.sum(error[:, None] * mixed[i], axis=0)
        term_w = term_w + lax.dot_general(
            s_rows[i],
            dcross.astype(jnp.bfloat16),
            (((0,), (0,)), ((), ())),
            preferred_element_type=jnp.float32,
        )

    small = jnp.pad(jnp.stack([term_b, term_o]), ((0, 6), (0, 0)))
    parts = term_w.reshape(2, 8, 4, 2, 8, half_s).transpose(3, 0, 2, 1, 4, 5).reshape(16, 8, 8, half_s)
    parts = jnp.concatenate([parts, jnp.broadcast_to(small, (16, 1, 8, half_s))], axis=1)
    parts = lax.all_to_all(parts, ("group", "fsdp_0", "fsdp_2"), 0, 0, tiled=True).sum(axis=0)
    small = parts[8, :2].reshape(8, half_s // 4)
    parts = jnp.concatenate(
        [parts[:8], jnp.broadcast_to(small, (8, *small.shape))], axis=2
    )
    parts = lax.all_to_all(parts, "fsdp_1", 0, 0, tiled=True).sum(axis=0)
    got = [
        lax.ppermute(parts, ("group", "fsdp_3"), pairs)
        for pairs in (((0, 0), (1, 2), (2, 1), (3, 3)), ((0, 2), (1, 0), (2, 3), (3, 1)))
    ]
    low = jnp.where(group == 0, got[0], got[1])
    high = jnp.where(group == 0, got[1], got[0])
    grad_cross = jnp.concatenate([low[:, :half_s], high[:, :half_s]], axis=1)
    small = jnp.concatenate(
        [low[:, half_s:].reshape(2, half_s), high[:, half_s:].reshape(2, half_s)], axis=1
    )
    return grad_cross, small[0], small[1]


def solution(mesh):
    split = Mesh(mesh.devices.reshape(2, 2, 8, 4, 2), GROUP_FSDP)
    in_specs = (
        P(GROUP_FSDP, None),
        P(GROUP_FSDP, None),
        P(GROUP_FSDP),
        P(None, GROUP_FSDP),
        P(),
        P(),
        P(),
        P(),
        P(),
        P(),
    )
    out_specs = (P(FSDP, None), P(), P())
    return jax.shard_map(
        shards, mesh=split, in_specs=in_specs, out_specs=out_specs, check_vma=False
    )
```

```python
import math

import jax
import jax.numpy as jnp
from jax import lax
from jax.experimental import pallas as pl
from jax.experimental.pallas import tpu as pltpu
from jax.sharding import Mesh
from jax.sharding import PartitionSpec as P

FSDP = ("fsdp_0", "fsdp_1", "fsdp_2", "fsdp_3")
GROUP_FSDP = ("group", "fsdp_0", "fsdp_1", "fsdp_2", "fsdp_3")
SIZES = (4, 8, 4, 2)
Y, Z, X = 0, 1, 2


epsilon = 1e-06

Z_ORDER = (0, -1, 1, -2, 2, -3, 3, 4)
RING_ORDER = (0, -1, 1, 2)
SUM_ORDER = (2, -1, 1, 0)


def flat(y, z, x, c):
    return ((y * SIZES[1] + z) * SIZES[2] + x) * SIZES[3] + c


def shift_pairs(dims, step):
    pairs = []
    for y in range(SIZES[0]):
        for z in range(SIZES[1]):
            for x in range(SIZES[2]):
                for c in range(SIZES[3]):
                    to = [y, z, x, c]
                    to[dims[c]] = (to[dims[c]] + step) % SIZES[dims[c]]
                    pairs.append((flat(y, z, x, c), flat(*to)))
    return pairs


def shift(value, dims, step):
    return lax.ppermute(value, GROUP_FSDP, shift_pairs(dims, step))


def swap_cores(value):
    return lax.ppermute(value, "fsdp_3", ((0, 1), (1, 0)))


def join_kernel(*refs):
    out = refs[-1]
    at = 0
    for ref in refs[:-1]:
        size = ref.shape[0]
        out[at : at + size, :] = ref[...]
        at += size


def join(parts):
    rows = sum(p.shape[0] for p in parts)
    return pl.pallas_call(
        join_kernel,
        out_shape=jax.ShapeDtypeStruct((rows, parts[0].shape[1]), parts[0].dtype),
        name="join",
    )(*parts)


def ring_gather(first, second, dims):
    l1, r1 = shift(first, dims, 1), shift(first, dims, -1)
    l2, r2 = shift(second, dims, 1), shift(second, dims, -1)
    return (first, second), (l1, l2), (r1, r2), (shift(l1, dims, 1), shift(r2, dims, -1))


def ring_sum(opposite, left, right, own, dims):
    half = own.shape[0] // 2
    from_left = shift(right[half:], dims, 1)
    from_right = shift(left[:half], dims, -1)
    for_right = shift(opposite[:half], dims, 1)
    for_left = shift(opposite[half:], dims, -1)
    from_left_top = shift(right[:half] + for_right, dims, 1)
    from_right_end = shift(left[half:] + for_left, dims, -1)
    return jnp.concatenate(
        [own[:half] + from_right + from_left_top, own[half:] + from_left + from_right_end], axis=0
    )


def one_hot_rows(index, width, dtype):
    return (index[:, None] == lax.broadcasted_iota(jnp.int32, (1, width), 1)).astype(dtype)


def transposed_dot(left, right):
    return lax.dot_general(
        left, right, (((1,), (1,)), ((), ())), preferred_element_type=jnp.float32
    )


def shards(
    teacher_rows,
    student_rows,
    counts,
    teacher_weight,
    teacher_bias,
    teacher_gain,
    teacher_head,
    cross_weight,
    cross_bias,
    out_weight,
):
    rows = teacher_rows.shape[0]
    width_t = teacher_bias.shape[0]
    width_s = cross_weight.shape[0]
    half_s = width_s // 2
    local = teacher_weight.shape[1]
    loss_scale = math.sqrt(width_s / (rows * lax.axis_size(GROUP_FSDP)))
    y_at, z_at = lax.axis_index(("group", "fsdp_0")), lax.axis_index("fsdp_1")
    x_at, core = lax.axis_index("fsdp_2"), lax.axis_index("fsdp_3")
    group = lax.axis_index("group")

    mine = teacher_weight.T
    z_axis = (Z, Z)
    m1, p1 = shift(mine, z_axis, 1), shift(mine, z_axis, -1)
    m2, p2 = shift(mine, z_axis, 2), shift(mine, z_axis, -2)
    m3, p3, far = shift(m2, z_axis, 1), shift(p2, z_axis, -1), shift(m2, z_axis, 2)

    t_rows = jnp.concatenate([teacher_rows, swap_cores(teacher_rows)], axis=0)
    s_rows = jnp.concatenate([student_rows, swap_cores(student_rows)], axis=0)

    vectors = jnp.stack([teacher_bias, teacher_gain, teacher_head]).reshape(3, 4, 8 * 4 * 2 * local)
    order_y = (y_at + jnp.array(RING_ORDER, jnp.int32)) % 4
    order_x = (x_at + jnp.array(RING_ORDER, jnp.int32)) % 4
    order_z = (z_at + jnp.array(Z_ORDER, jnp.int32)) % 8
    units = (
        order_z[None, :, None] * (8 * local)
        + order_x[:, None, None] * (2 * local)
        + core * local
        + jnp.arange(local, dtype=jnp.int32)[None, None, :]
    ).reshape(-1)
    exact = lax.Precision.HIGHEST
    vectors = jnp.einsum(
        "wy,vyk->vwk", one_hot_rows(order_y, 4, jnp.float32), vectors, precision=exact
    )
    vectors = lax.dot_general(
        vectors.reshape(12, -1),
        one_hot_rows(units, vectors.shape[2], jnp.float32),
        (((1,), (1,)), ((), ())),
        precision=exact,
    ).reshape(3, 4, 4, 8 * local)
    vectors = jnp.where(core == 0, vectors, vectors.transpose(0, 2, 1, 3))

    near, wide = (X, Y), (Y, X)
    low, high = join([mine, m1, p1, m2]), join([p2, m3, p3, far])
    low, high, vectors, t_rows = lax.optimization_barrier((low, high, vectors, t_rows))
    own, left, right, opposite = ring_gather(low, high, near)
    plane_a, plane_b = join([*own, *left]), join([*right, *opposite])

    cut = core * half_s
    cross_half = lax.dynamic_slice_in_dim(cross_weight, cut, half_s, axis=1)
    cross_bias_half = lax.dynamic_slice_in_dim(cross_bias, cut, half_s)
    out_half = lax.dynamic_slice_in_dim(out_weight, cut, half_s)
    cross = lax.dot_general(
        cross_half, s_rows, (((0,), (1,)), ((), ())), preferred_element_type=jnp.float32
    ) + cross_bias_half[:, None]
    inputs = transposed_dot(
        one_hot_rows(cut + jnp.arange(half_s, dtype=jnp.int32), width_s, s_rows.dtype), s_rows
    )
    mixed = inputs * cross + inputs
    student_part = jnp.sum(mixed * out_half[:, None], axis=0)

    sum_y = (y_at + jnp.array(SUM_ORDER, jnp.int32)) % 4
    sum_x = (x_at + jnp.array(SUM_ORDER, jnp.int32)) % 4
    base_y = (sum_y % 2) * (8 * 4 * 16) + (sum_y // 2) * 8
    base_x = sum_x * 16
    base = jnp.where(
        core == 0, base_x[:, None] + base_y[None, :], base_y[:, None] + base_x[None, :]
    )
    features = (
        base[:, :, None, None]
        + jnp.arange(8, dtype=jnp.int32)[:, None] * (4 * 16)
        + jnp.arange(8, dtype=jnp.int32)[None, :]
    ).reshape(-1)
    turned = transposed_dot(one_hot_rows(features, width_s, s_rows.dtype), s_rows).astype(
        s_rows.dtype
    )
    plane_b, inputs, mixed, student_part, turned = lax.optimization_barrier(
        (plane_b, inputs, mixed, student_part, turned)
    )
    blocks = ring_gather(plane_a, plane_b, wide)

    units = plane_a.shape[0]
    pieces = [(i, j) for i, j in ((0, 0), (0, 1), (1, 0), (2, 0), (1, 1), (2, 1), (3, 0), (3, 1))]
    preact, squares = {}, 0.0
    for i, j in pieces:
        bias = vectors[0, i, 2 * j : 2 * j + 2].reshape(units)
        p = transposed_dot(blocks[i][j], t_rows) + bias[:, None]
        preact[i, j] = p
        squares = squares + jnp.sum(p * p, axis=0)

    amount = counts.astype(jnp.float32)
    other = swap_cores(jnp.concatenate([squares, jnp.broadcast_to(amount, (128,))]))
    squares = squares + jnp.concatenate([other[rows : 2 * rows], other[:rows]])
    amounts = jnp.concatenate(
        [jnp.broadcast_to(amount, (rows,)), jnp.broadcast_to(other[2 * rows], (rows,))]
    )

    scale = lax.rsqrt(squares / width_t + epsilon)[None, :]
    logit = 0.0
    for i, j in pieces:
        gain, head = (vectors[k, i, 2 * j : 2 * j + 2].reshape(units)[:, None] for k in (1, 2))
        normed = preact[i, j] * scale * gain
        gated = 0.5 * normed * (1.0 + jnp.tanh(0.5 * normed))
        logit = logit + jnp.sum(gated * head, axis=0)
    part = student_part - logit
    other = swap_cores(part)
    differ = part + jnp.concatenate([other[rows:], other[:rows]])
    place = (jnp.arange(2 * rows, dtype=jnp.int32) % rows).astype(jnp.float32)
    error = (differ * (place < amounts).astype(jnp.float32) * loss_scale)[None, :]
    dcross = error * out_half[:, None] * inputs
    dcross_half = dcross.astype(jnp.bfloat16)
    small = jnp.stack([jnp.sum(dcross, axis=1), jnp.sum(error * mixed, axis=1)])

    quarter = width_s // 4
    opposite = transposed_dot(turned[:quarter], dcross_half)
    rest = transposed_dot(turned[quarter:], dcross_half)
    parts = ring_sum(opposite, *(rest[i * quarter : (i + 1) * quarter] for i in range(3)), near)
    eighth = quarter // 4
    parts = ring_sum(*(parts[i * eighth : (i + 1) * eighth] for i in range(4)), wide)
    small = jnp.broadcast_to(small.reshape(1, 8, half_s // 4), (16, 8, half_s // 4))
    small = lax.all_to_all(small, ("group", "fsdp_0", "fsdp_2"), 0, 0, tiled=True).sum(axis=0)
    parts = jnp.concatenate(
        [parts.reshape(8, 8, half_s), jnp.broadcast_to(small, (8, *small.shape))], axis=2
    )
    parts = lax.all_to_all(parts, "fsdp_1", 0, 0, tiled=True).sum(axis=0)
    got = [
        lax.ppermute(parts, ("group", "fsdp_3"), pairs)
        for pairs in (((0, 0), (1, 2), (2, 1), (3, 3)), ((0, 2), (1, 0), (2, 3), (3, 1)))
    ]
    low = jnp.where(group == 0, got[0], got[1])
    high = jnp.where(group == 0, got[1], got[0])
    grad_cross = jnp.concatenate([low[:, :half_s], high[:, :half_s]], axis=1)
    small = jnp.concatenate(
        [low[:, half_s:].reshape(2, half_s), high[:, half_s:].reshape(2, half_s)], axis=1
    )
    return grad_cross, small[0], small[1]


def solution(mesh):
    split = Mesh(mesh.devices.reshape(2, 2, 8, 4, 2), GROUP_FSDP)
    in_specs = (
        P(GROUP_FSDP, None),
        P(GROUP_FSDP, None),
        P(GROUP_FSDP),
        P(None, GROUP_FSDP),
        P(),
        P(),
        P(),
        P(),
        P(),
        P(),
    )
    out_specs = (P(FSDP, None), P(), P())
    return jax.shard_map(
        shards, mesh=split, in_specs=in_specs, out_specs=out_specs, check_vma=False
    )
```

```python
import math

import jax
import jax.numpy as jnp
from jax import lax
from jax.experimental import pallas as pl
from jax.sharding import Mesh
from jax.sharding import PartitionSpec as P

FSDP = ("fsdp_0", "fsdp_1", "fsdp_2", "fsdp_3")
GROUP_FSDP = ("group", "fsdp_0", "fsdp_1", "fsdp_2", "fsdp_3")
SIZES = (4, 8, 4, 2)
Y, X = 0, 2


epsilon = 1e-06

RING_ORDER = (0, -1, 1, 2)


def flat(y, z, x, c):
    return ((y * SIZES[1] + z) * SIZES[2] + x) * SIZES[3] + c


def shift_pairs(dims, step):
    pairs = []
    for y in range(SIZES[0]):
        for z in range(SIZES[1]):
            for x in range(SIZES[2]):
                for c in range(SIZES[3]):
                    to = [y, z, x, c]
                    to[dims[c]] = (to[dims[c]] + step) % SIZES[dims[c]]
                    pairs.append((flat(y, z, x, c), flat(*to)))
    return pairs


def shift(value, dims, step):
    return lax.ppermute(value, GROUP_FSDP, shift_pairs(dims, step))


def swap_cores(value):
    return lax.ppermute(value, "fsdp_3", ((0, 1), (1, 0)))


def join_kernel(*refs):
    out = refs[-1]
    at = 0
    for ref in refs[:-1]:
        size = ref.shape[0]
        out[at : at + size, :] = ref[...]
        at += size


def join(parts):
    rows = sum(p.shape[0] for p in parts)
    return pl.pallas_call(
        join_kernel,
        out_shape=jax.ShapeDtypeStruct((rows, parts[0].shape[1]), parts[0].dtype),
        name="join",
    )(*parts)


def ring_gather(block, dims, way):
    left = shift(block, dims, 1)
    right = shift(block, dims, -1)
    far = shift(left if way == 1 else right, dims, way)
    return block, left, right, far


def one_hot_rows(index, width, dtype):
    return (index[:, None] == lax.broadcasted_iota(jnp.int32, (1, width), 1)).astype(dtype)


def transposed_dot(left, right):
    return lax.dot_general(
        left, right, (((1,), (1,)), ((), ())), preferred_element_type=jnp.float32
    )


def shards(
    teacher_rows,
    student_rows,
    counts,
    teacher_weight,
    teacher_bias,
    teacher_gain,
    teacher_head,
    cross_weight,
    cross_bias,
    out_weight,
):
    rows = teacher_rows.shape[0]
    width_t = teacher_bias.shape[0]
    width_s = cross_weight.shape[0]
    half_s = width_s // 2
    local = teacher_weight.shape[1]
    loss_scale = math.sqrt(width_s / (rows * lax.axis_size(GROUP_FSDP)))
    y_at = lax.axis_index(("group", "fsdp_0"))
    x_at, core = lax.axis_index("fsdp_2"), lax.axis_index("fsdp_3")
    group = lax.axis_index("group")

    mine = teacher_weight.T.reshape(2, local // 2, -1)
    lines = []
    for i in range(2):
        lines.append(
            lax.all_to_all(
                jnp.broadcast_to(mine[i][None], (8, *mine.shape[1:])), "fsdp_1", 0, 0, tiled=True
            ).reshape(4 * local, -1)
        )

    t_rows = jnp.concatenate([teacher_rows, swap_cores(teacher_rows)], axis=0)
    s_rows = jnp.concatenate([student_rows, swap_cores(student_rows)], axis=0)

    vectors = jnp.stack([teacher_bias, teacher_gain, teacher_head]).reshape(3, 4, 8 * 4 * 2 * local)
    order_y = (y_at + jnp.array(RING_ORDER, jnp.int32)) % 4
    order_x = (x_at + jnp.array(RING_ORDER, jnp.int32)) % 4
    units = (
        jnp.arange(2, dtype=jnp.int32)[:, None, None, None] * (local // 2)
        + order_x[None, :, None, None] * (2 * local)
        + jnp.arange(8, dtype=jnp.int32)[None, None, :, None] * (8 * local)
        + core * local
        + jnp.arange(local // 2, dtype=jnp.int32)[None, None, None, :]
    ).reshape(-1)
    exact = lax.Precision.HIGHEST
    vectors = jnp.einsum(
        "wy,vyk->vwk", one_hot_rows(order_y, 4, jnp.float32), vectors, precision=exact
    )
    vectors = lax.dot_general(
        vectors.reshape(12, -1),
        one_hot_rows(units, vectors.shape[2], jnp.float32),
        (((1,), (1,)), ((), ())),
        precision=exact,
    ).reshape(3, 4, 2, 4, 4 * local)
    vectors = jnp.where(core == 0, vectors, vectors.transpose(0, 3, 2, 1, 4))
    vectors = vectors.reshape(3, 4, 2, 16 * local)

    near, wide = (X, Y), (Y, X)
    plane_a = join(ring_gather(lines[0], near, 1))
    plane_b = join(ring_gather(lines[1], near, -1))
    plane_a, vectors, t_rows = lax.optimization_barrier((plane_a, vectors, t_rows))

    cut = core * half_s
    cross_half = lax.dynamic_slice_in_dim(cross_weight, cut, half_s, axis=1)
    cross_bias_half = lax.dynamic_slice_in_dim(cross_bias, cut, half_s)
    out_half = lax.dynamic_slice_in_dim(out_weight, cut, half_s)
    cross = lax.dot_general(
        cross_half, s_rows, (((0,), (1,)), ((), ())), preferred_element_type=jnp.float32
    ) + cross_bias_half[:, None]
    inputs = transposed_dot(
        one_hot_rows(cut + jnp.arange(half_s, dtype=jnp.int32), width_s, s_rows.dtype), s_rows
    )
    mixed = inputs * cross + inputs
    student_part = jnp.sum(mixed * out_half[:, None], axis=0)

    features = (
        jnp.arange(2, dtype=jnp.int32)[:, None, None, None, None] * 8
        + jnp.arange(2, dtype=jnp.int32)[:, None, None, None] * (8 * 4 * 16)
        + jnp.arange(4, dtype=jnp.int32)[:, None, None] * 16
        + jnp.arange(8, dtype=jnp.int32)[:, None] * (4 * 16)
        + jnp.arange(8, dtype=jnp.int32)
    ).reshape(-1)
    turned = transposed_dot(one_hot_rows(features, width_s, s_rows.dtype), s_rows).astype(
        s_rows.dtype
    )
    wide_a = ring_gather(plane_a, wide, 1)
    wide_b = ring_gather(plane_b, wide, -1)
    last, inputs, mixed, student_part, turned = lax.optimization_barrier(
        (wide_b[3], inputs, mixed, student_part, turned)
    )
    blocks = wide_a, (*wide_b[:3], last)

    pieces = [(i, j) for i in range(4) for j in range(2)]
    preact, squares = {}, 0.0
    for i, j in pieces:
        p = transposed_dot(blocks[j][i], t_rows) + vectors[0, i, j][:, None]
        preact[i, j] = p
        squares = squares + jnp.sum(p * p, axis=0)

    amount = counts.astype(jnp.float32)
    other = swap_cores(jnp.concatenate([squares, jnp.broadcast_to(amount, (128,))]))
    squares = squares + jnp.concatenate([other[rows : 2 * rows], other[:rows]])
    amounts = jnp.concatenate(
        [jnp.broadcast_to(amount, (rows,)), jnp.broadcast_to(other[2 * rows], (rows,))]
    )

    scale = lax.rsqrt(squares / width_t + epsilon)[None, :]
    logit = 0.0
    for i, j in pieces:
        gain, head = vectors[1, i, j][:, None], vectors[2, i, j][:, None]
        normed = preact[i, j] * scale * gain
        gated = 0.5 * normed * (1.0 + jnp.tanh(0.5 * normed))
        logit = logit + jnp.sum(gated * head, axis=0)
    part = student_part - logit
    other = swap_cores(part)
    differ = part + jnp.concatenate([other[rows:], other[:rows]])
    place = (jnp.arange(2 * rows, dtype=jnp.int32) % rows).astype(jnp.float32)
    error = (differ * (place < amounts).astype(jnp.float32) * loss_scale)[None, :]
    dcross = error * out_half[:, None] * inputs
    dcross_half = dcross.astype(jnp.bfloat16)
    small = jnp.stack([jnp.sum(dcross, axis=1), jnp.sum(error * mixed, axis=1)])

    parts = transposed_dot(turned, dcross_half).reshape(16, 8, 8, half_s)
    small = jnp.broadcast_to(jnp.pad(small, ((0, 6), (0, 0))), (16, 1, 8, half_s))
    parts = jnp.concatenate([parts, small], axis=1)
    parts = lax.all_to_all(parts, ("group", "fsdp_0", "fsdp_2"), 0, 0, tiled=True).sum(axis=0)
    small = parts[8, :2].reshape(8, half_s // 4)
    parts = jnp.concatenate(
        [parts[:8], jnp.broadcast_to(small, (8, *small.shape))], axis=2
    )
    parts = lax.all_to_all(parts, "fsdp_1", 0, 0, tiled=True).sum(axis=0)
    got = [
        lax.ppermute(parts, ("group", "fsdp_3"), pairs)
        for pairs in (((0, 0), (1, 2), (2, 1), (3, 3)), ((0, 2), (1, 0), (2, 3), (3, 1)))
    ]
    low = jnp.where(group == 0, got[0], got[1])
    high = jnp.where(group == 0, got[1], got[0])
    grad_cross = jnp.concatenate([low[:, :half_s], high[:, :half_s]], axis=1)
    small = jnp.concatenate(
        [low[:, half_s:].reshape(2, half_s), high[:, half_s:].reshape(2, half_s)], axis=1
    )
    return grad_cross, small[0], small[1]


def solution(mesh):
    split = Mesh(mesh.devices.reshape(2, 2, 8, 4, 2), GROUP_FSDP)
    in_specs = (
        P(GROUP_FSDP, None),
        P(GROUP_FSDP, None),
        P(GROUP_FSDP),
        P(None, GROUP_FSDP),
        P(),
        P(),
        P(),
        P(),
        P(),
        P(),
    )
    out_specs = (P(FSDP, None), P(), P())
    return jax.shard_map(
        shards,
        mesh=split,
        in_specs=in_specs,
        out_specs=out_specs,
        check_vma=False,
    )
```

```python
import math

import jax
import jax.numpy as jnp
from jax import lax
from jax.experimental import pallas as pl
from jax.sharding import Mesh
from jax.sharding import PartitionSpec as P

FSDP = ("fsdp_0", "fsdp_1", "fsdp_2", "fsdp_3")
GROUP_FSDP = ("group", "fsdp_0", "fsdp_1", "fsdp_2", "fsdp_3")
SIZES = (4, 8, 4, 2)
Y, X = 0, 2


epsilon = 1e-06

RING_ORDER = (0, -1, 1, 2)


def flat(y, z, x, c):
    return ((y * SIZES[1] + z) * SIZES[2] + x) * SIZES[3] + c


def shift_pairs(dims, step):
    pairs = []
    for y in range(SIZES[0]):
        for z in range(SIZES[1]):
            for x in range(SIZES[2]):
                for c in range(SIZES[3]):
                    to = [y, z, x, c]
                    to[dims[c]] = (to[dims[c]] + step) % SIZES[dims[c]]
                    pairs.append((flat(y, z, x, c), flat(*to)))
    return pairs


def shift(value, dims, step):
    return lax.ppermute(value, GROUP_FSDP, shift_pairs(dims, step))


def swap_cores(value):
    return lax.ppermute(value, "fsdp_3", ((0, 1), (1, 0)))


def join_kernel(*refs):
    out = refs[-1]
    at = 0
    for ref in refs[:-1]:
        size = ref.shape[0]
        out[at : at + size, :] = ref[...]
        at += size


def join(parts):
    rows = sum(p.shape[0] for p in parts)
    return pl.pallas_call(
        join_kernel,
        out_shape=jax.ShapeDtypeStruct((rows, parts[0].shape[1]), parts[0].dtype),
        name="join",
    )(*parts)


def ring_gather(block, dims):
    left, right = shift(block, dims, 1), shift(block, dims, -1)
    return block, left, right, shift(left, dims, 1)


def wide_gather(first, second, dims):
    l1, r1 = shift(first, dims, 1), shift(first, dims, -1)
    l2, r2 = shift(second, dims, 1), shift(second, dims, -1)
    far = shift(l1, dims, 1), shift(r2, dims, -1)
    return (first, second), (l1, l2), (r1, r2), far


def one_hot_rows(index, width, dtype):
    return (index[:, None] == lax.broadcasted_iota(jnp.int32, (1, width), 1)).astype(dtype)


def transposed_dot(left, right):
    return lax.dot_general(
        left, right, (((1,), (1,)), ((), ())), preferred_element_type=jnp.float32
    )


def shards(
    teacher_rows,
    student_rows,
    counts,
    teacher_weight,
    teacher_bias,
    teacher_gain,
    teacher_head,
    cross_weight,
    cross_bias,
    out_weight,
):
    rows = teacher_rows.shape[0]
    width_t = teacher_bias.shape[0]
    width_s = cross_weight.shape[0]
    half_s = width_s // 2
    local = teacher_weight.shape[1]
    loss_scale = math.sqrt(width_s / (rows * lax.axis_size(GROUP_FSDP)))
    y_at = lax.axis_index(("group", "fsdp_0"))
    x_at, core = lax.axis_index("fsdp_2"), lax.axis_index("fsdp_3")
    group = lax.axis_index("group")

    mine = teacher_weight.T
    line = lax.all_to_all(
        jnp.broadcast_to(mine[None], (8, *mine.shape)), "fsdp_1", 0, 0, tiled=True
    ).reshape(8 * local, -1)

    t_rows = jnp.concatenate([teacher_rows, swap_cores(teacher_rows)], axis=0)
    s_rows = jnp.concatenate([student_rows, swap_cores(student_rows)], axis=0)

    vectors = jnp.stack([teacher_bias, teacher_gain, teacher_head]).reshape(3, 4, 8 * 4 * 2 * local)
    order_y = (y_at + jnp.array(RING_ORDER, jnp.int32)) % 4
    order_x = (x_at + jnp.array(RING_ORDER, jnp.int32)) % 4
    units = (
        order_x[:, None, None] * (2 * local)
        + jnp.arange(8, dtype=jnp.int32)[None, :, None] * (8 * local)
        + core * local
        + jnp.arange(local, dtype=jnp.int32)[None, None, :]
    ).reshape(-1)
    exact = lax.Precision.HIGHEST
    vectors = jnp.einsum(
        "wy,vyk->vwk", one_hot_rows(order_y, 4, jnp.float32), vectors, precision=exact
    )
    vectors = lax.dot_general(
        vectors.reshape(12, -1),
        one_hot_rows(units, vectors.shape[2], jnp.float32),
        (((1,), (1,)), ((), ())),
        precision=exact,
    ).reshape(3, 4, 4, 8 * local)
    vectors = jnp.where(core == 0, vectors, vectors.transpose(0, 2, 1, 3))
    vectors = vectors.reshape(3, 4, 2, 16 * local)
    line, vectors, t_rows, s_rows = lax.optimization_barrier((line, vectors, t_rows, s_rows))

    near, wide = (X, Y), (Y, X)
    around = ring_gather(line, near)
    plane = join(around[:2]), join(around[2:])

    cut = core * half_s
    cross_half = lax.dynamic_slice_in_dim(cross_weight, cut, half_s, axis=1)
    cross_bias_half = lax.dynamic_slice_in_dim(cross_bias, cut, half_s)
    out_half = lax.dynamic_slice_in_dim(out_weight, cut, half_s)
    cross = lax.dot_general(
        cross_half, s_rows, (((0,), (1,)), ((), ())), preferred_element_type=jnp.float32
    ) + cross_bias_half[:, None]
    inputs = transposed_dot(
        one_hot_rows(cut + jnp.arange(half_s, dtype=jnp.int32), width_s, s_rows.dtype), s_rows
    )
    mixed = inputs * cross + inputs
    student_part = jnp.sum(mixed * out_half[:, None], axis=0)

    features = (
        jnp.arange(2, dtype=jnp.int32)[:, None, None, None, None] * 8
        + jnp.arange(2, dtype=jnp.int32)[:, None, None, None] * (8 * 4 * 16)
        + jnp.arange(4, dtype=jnp.int32)[:, None, None] * 16
        + jnp.arange(8, dtype=jnp.int32)[:, None] * (4 * 16)
        + jnp.arange(8, dtype=jnp.int32)
    ).reshape(-1)
    turned = transposed_dot(one_hot_rows(features, width_s, s_rows.dtype), s_rows).astype(
        s_rows.dtype
    )
    blocks = wide_gather(*plane, wide)
    last, inputs, mixed, student_part, turned = lax.optimization_barrier(
        (blocks[3][1], inputs, mixed, student_part, turned)
    )
    blocks = (*blocks[:3], (blocks[3][0], last))

    pieces = [(i, j) for i in range(4) for j in range(2)]
    preact, squares = {}, 0.0
    for i, j in pieces:
        p = transposed_dot(blocks[i][j], t_rows) + vectors[0, i, j][:, None]
        preact[i, j] = p
        squares = squares + jnp.sum(p * p, axis=0)

    amount = counts.astype(jnp.float32)
    other = swap_cores(jnp.concatenate([squares, jnp.broadcast_to(amount, (128,))]))
    squares = squares + jnp.concatenate([other[rows : 2 * rows], other[:rows]])
    amounts = jnp.concatenate(
        [jnp.broadcast_to(amount, (rows,)), jnp.broadcast_to(other[2 * rows], (rows,))]
    )

    scale = lax.rsqrt(squares / width_t + epsilon)[None, :]
    logit = 0.0
    for i, j in pieces:
        gain, head = vectors[1, i, j][:, None], vectors[2, i, j][:, None]
        normed = preact[i, j] * scale * gain
        gated = 0.5 * normed * (1.0 + jnp.tanh(0.5 * normed))
        logit = logit + jnp.sum(gated * head, axis=0)
    part = student_part - logit
    other = swap_cores(part)
    differ = part + jnp.concatenate([other[rows:], other[:rows]])
    place = (jnp.arange(2 * rows, dtype=jnp.int32) % rows).astype(jnp.float32)
    error = (differ * (place < amounts).astype(jnp.float32) * loss_scale)[None, :]
    dcross = error * out_half[:, None] * inputs
    dcross_half = dcross.astype(jnp.bfloat16)
    small = jnp.stack([jnp.sum(dcross, axis=1), jnp.sum(error * mixed, axis=1)])

    parts = transposed_dot(turned, dcross_half).reshape(16, 8, 8, half_s)
    small = jnp.broadcast_to(jnp.pad(small, ((0, 6), (0, 0))), (16, 1, 8, half_s))
    parts = jnp.concatenate([parts, small], axis=1)
    parts = lax.all_to_all(parts, ("group", "fsdp_0", "fsdp_2"), 0, 0, tiled=True).sum(axis=0)
    small = parts[8, :2].reshape(8, half_s // 4)
    parts = jnp.concatenate(
        [parts[:8], jnp.broadcast_to(small, (8, *small.shape))], axis=2
    )
    parts = lax.all_to_all(parts, "fsdp_1", 0, 0, tiled=True).sum(axis=0)
    got = [
        lax.ppermute(parts, ("group", "fsdp_3"), pairs)
        for pairs in (((0, 0), (1, 2), (2, 1), (3, 3)), ((0, 2), (1, 0), (2, 3), (3, 1)))
    ]
    low = jnp.where(group == 0, got[0], got[1])
    high = jnp.where(group == 0, got[1], got[0])
    grad_cross = jnp.concatenate([low[:, :half_s], high[:, :half_s]], axis=1)
    small = jnp.concatenate(
        [low[:, half_s:].reshape(2, half_s), high[:, half_s:].reshape(2, half_s)], axis=1
    )
    return grad_cross, small[0], small[1]


def solution(mesh):
    split = Mesh(mesh.devices.reshape(2, 2, 8, 4, 2), GROUP_FSDP)
    in_specs = (
        P(GROUP_FSDP, None),
        P(GROUP_FSDP, None),
        P(GROUP_FSDP),
        P(None, GROUP_FSDP),
        P(),
        P(),
        P(),
        P(),
        P(),
        P(),
    )
    out_specs = (P(FSDP, None), P(), P())
    return jax.shard_map(
        shards,
        mesh=split,
        in_specs=in_specs,
        out_specs=out_specs,
        check_vma=False,
    )
```

```python
import math

import jax
import jax.numpy as jnp
from jax import lax
from jax.experimental import pallas as pl
from jax.sharding import Mesh
from jax.sharding import PartitionSpec as P

FSDP = ("fsdp_0", "fsdp_1", "fsdp_2", "fsdp_3")
GROUP_FSDP = ("group", "fsdp_0", "fsdp_1", "fsdp_2", "fsdp_3")
SIZES = (4, 8, 4, 2)
Y, X = 0, 2


epsilon = 1e-06

RING_ORDER = (0, -1, 1, 2)


def flat(y, z, x, c):
    return ((y * SIZES[1] + z) * SIZES[2] + x) * SIZES[3] + c


def shift_pairs(dims, step):
    pairs = []
    for y in range(SIZES[0]):
        for z in range(SIZES[1]):
            for x in range(SIZES[2]):
                for c in range(SIZES[3]):
                    to = [y, z, x, c]
                    to[dims[c]] = (to[dims[c]] + step) % SIZES[dims[c]]
                    pairs.append((flat(y, z, x, c), flat(*to)))
    return pairs


def shift(value, dims, step):
    return lax.ppermute(value, GROUP_FSDP, shift_pairs(dims, step))


def swap_cores(value):
    return lax.ppermute(value, "fsdp_3", ((0, 1), (1, 0)))


def join_kernel(*refs):
    out = refs[-1]
    at = 0
    for ref in refs[:-1]:
        size = ref.shape[0]
        out[at : at + size, :] = ref[...]
        at += size


def join(parts):
    rows = sum(p.shape[0] for p in parts)
    return pl.pallas_call(
        join_kernel,
        out_shape=jax.ShapeDtypeStruct((rows, parts[0].shape[1]), parts[0].dtype),
        name="join",
    )(*parts)


def ring_gather(block, dims):
    left, right = shift(block, dims, 1), shift(block, dims, -1)
    return block, left, right, shift(left, dims, 1)


def wide_gather(first, second, dims):
    l1, r1 = shift(first, dims, 1), shift(first, dims, -1)
    l2, r2 = shift(second, dims, 1), shift(second, dims, -1)
    far = shift(l1, dims, 1), shift(r2, dims, -1)
    return (first, second), (l1, l2), (r1, r2), far


def line_sum(parts, dims):
    groups = {}
    for index in range(math.prod(SIZES)):
        at = [index // 64, index // 8 % 8, index // 2 % 4, index % 2]
        at[dims[at[3]]] = -1
        groups.setdefault(tuple(at), []).append(index)
    return lax.all_to_all(
        parts, GROUP_FSDP, 0, 0, axis_index_groups=list(groups.values()), tiled=True
    ).sum(axis=0)


def one_hot_rows(index, width, dtype):
    return (index[:, None] == lax.broadcasted_iota(jnp.int32, (1, width), 1)).astype(dtype)


def transposed_dot(left, right):
    return lax.dot_general(
        left, right, (((1,), (1,)), ((), ())), preferred_element_type=jnp.float32
    )


def shards(
    teacher_rows,
    student_rows,
    counts,
    teacher_weight,
    teacher_bias,
    teacher_gain,
    teacher_head,
    cross_weight,
    cross_bias,
    out_weight,
):
    rows = teacher_rows.shape[0]
    width_t = teacher_bias.shape[0]
    width_s = cross_weight.shape[0]
    half_s = width_s // 2
    local = teacher_weight.shape[1]
    loss_scale = math.sqrt(width_s / (rows * lax.axis_size(GROUP_FSDP)))
    y_at = lax.axis_index(("group", "fsdp_0"))
    x_at, core = lax.axis_index("fsdp_2"), lax.axis_index("fsdp_3")
    group = lax.axis_index("group")

    mine = teacher_weight.T
    line = lax.all_to_all(
        jnp.broadcast_to(mine[None], (8, *mine.shape)), "fsdp_1", 0, 0, tiled=True
    ).reshape(8 * local, -1)

    t_rows = jnp.concatenate([teacher_rows, swap_cores(teacher_rows)], axis=0)
    s_rows = jnp.concatenate([student_rows, swap_cores(student_rows)], axis=0)

    vectors = jnp.stack([teacher_bias, teacher_gain, teacher_head]).reshape(3, 4, 8 * 4 * 2 * local)
    order_y = (y_at + jnp.array(RING_ORDER, jnp.int32)) % 4
    order_x = (x_at + jnp.array(RING_ORDER, jnp.int32)) % 4
    units = (
        order_x[:, None, None] * (2 * local)
        + jnp.arange(8, dtype=jnp.int32)[None, :, None] * (8 * local)
        + core * local
        + jnp.arange(local, dtype=jnp.int32)[None, None, :]
    ).reshape(-1)
    exact = lax.Precision.HIGHEST
    vectors = jnp.einsum(
        "wy,vyk->vwk", one_hot_rows(order_y, 4, jnp.float32), vectors, precision=exact
    )
    vectors = lax.dot_general(
        vectors.reshape(12, -1),
        one_hot_rows(units, vectors.shape[2], jnp.float32),
        (((1,), (1,)), ((), ())),
        precision=exact,
    ).reshape(3, 4, 4, 8 * local)
    vectors = jnp.where(core == 0, vectors, vectors.transpose(0, 2, 1, 3))
    vectors = vectors.reshape(3, 4, 2, 16 * local)
    line, vectors, t_rows, s_rows = lax.optimization_barrier((line, vectors, t_rows, s_rows))

    near, wide = (X, Y), (Y, X)
    around = ring_gather(line, near)
    plane = join(around[:2]), join(around[2:])

    cut = core * half_s
    cross_half = lax.dynamic_slice_in_dim(cross_weight, cut, half_s, axis=1)
    cross_bias_half = lax.dynamic_slice_in_dim(cross_bias, cut, half_s)
    out_half = lax.dynamic_slice_in_dim(out_weight, cut, half_s)
    cross = lax.dot_general(
        cross_half, s_rows, (((0,), (1,)), ((), ())), preferred_element_type=jnp.float32
    ) + cross_bias_half[:, None]
    inputs = transposed_dot(
        one_hot_rows(cut + jnp.arange(half_s, dtype=jnp.int32), width_s, s_rows.dtype), s_rows
    )
    mixed = inputs * cross + inputs
    student_part = jnp.sum(mixed * out_half[:, None], axis=0)

    place_y = jnp.array([(y % 2) * (8 * 4 * 16) + (y // 2) * 8 for y in range(4)], jnp.int32)
    place_x = jnp.arange(4, dtype=jnp.int32) * 16
    features = (
        jnp.where(
            core == 0,
            place_x[:, None] + place_y[None, :],
            place_y[:, None] + place_x[None, :],
        )[:, :, None, None]
        + jnp.arange(8, dtype=jnp.int32)[:, None] * (4 * 16)
        + jnp.arange(8, dtype=jnp.int32)
    ).reshape(-1)
    turned = transposed_dot(one_hot_rows(features, width_s, s_rows.dtype), s_rows).astype(
        s_rows.dtype
    )
    blocks = wide_gather(*plane, wide)
    last, inputs, mixed, student_part, turned = lax.optimization_barrier(
        (blocks[3][1], inputs, mixed, student_part, turned)
    )
    blocks = (*blocks[:3], (blocks[3][0], last))

    pieces = [(i, j) for i in range(4) for j in range(2)]
    preact, squares = {}, 0.0
    for i, j in pieces:
        p = transposed_dot(blocks[i][j], t_rows) + vectors[0, i, j][:, None]
        preact[i, j] = p
        squares = squares + jnp.sum(p * p, axis=0)

    amount = counts.astype(jnp.float32)
    other = swap_cores(jnp.concatenate([squares, jnp.broadcast_to(amount, (128,))]))
    squares = squares + jnp.concatenate([other[rows : 2 * rows], other[:rows]])
    amounts = jnp.concatenate(
        [jnp.broadcast_to(amount, (rows,)), jnp.broadcast_to(other[2 * rows], (rows,))]
    )

    scale = lax.rsqrt(squares / width_t + epsilon)[None, :]
    logit = 0.0
    for i, j in pieces:
        gain, head = vectors[1, i, j][:, None], vectors[2, i, j][:, None]
        normed = preact[i, j] * scale * gain
        gated = 0.5 * normed * (1.0 + jnp.tanh(0.5 * normed))
        logit = logit + jnp.sum(gated * head, axis=0)
    part = student_part - logit
    other = swap_cores(part)
    differ = part + jnp.concatenate([other[rows:], other[:rows]])
    place = (jnp.arange(2 * rows, dtype=jnp.int32) % rows).astype(jnp.float32)
    error = (differ * (place < amounts).astype(jnp.float32) * loss_scale)[None, :]
    dcross = error * out_half[:, None] * inputs
    dcross_half = dcross.astype(jnp.bfloat16)
    small = jnp.stack([jnp.sum(dcross, axis=1), jnp.sum(error * mixed, axis=1)])

    parts = transposed_dot(turned, dcross_half).reshape(4, -1, half_s)
    small = jnp.broadcast_to(jnp.pad(small, ((0, 6), (0, 0))), (4, 8, half_s))
    parts = line_sum(jnp.concatenate([parts, small], axis=1), near)
    small = jnp.broadcast_to(parts[-8:], (4, 8, half_s))
    parts = line_sum(jnp.concatenate([parts[:-8].reshape(4, -1, half_s), small], axis=1), wide)
    parts = parts.reshape(9, 8, half_s)
    small = parts[8, :2].reshape(8, half_s // 4)
    parts = jnp.concatenate(
        [parts[:8], jnp.broadcast_to(small, (8, *small.shape))], axis=2
    )
    parts = lax.all_to_all(parts, "fsdp_1", 0, 0, tiled=True).sum(axis=0)
    got = [
        lax.ppermute(parts, ("group", "fsdp_3"), pairs)
        for pairs in (((0, 0), (1, 2), (2, 1), (3, 3)), ((0, 2), (1, 0), (2, 3), (3, 1)))
    ]
    low = jnp.where(group == 0, got[0], got[1])
    high = jnp.where(group == 0, got[1], got[0])
    grad_cross = jnp.concatenate([low[:, :half_s], high[:, :half_s]], axis=1)
    small = jnp.concatenate(
        [low[:, half_s:].reshape(2, half_s), high[:, half_s:].reshape(2, half_s)], axis=1
    )
    return grad_cross, small[0], small[1]


def solution(mesh):
    split = Mesh(mesh.devices.reshape(2, 2, 8, 4, 2), GROUP_FSDP)
    in_specs = (
        P(GROUP_FSDP, None),
        P(GROUP_FSDP, None),
        P(GROUP_FSDP),
        P(None, GROUP_FSDP),
        P(),
        P(),
        P(),
        P(),
        P(),
        P(),
    )
    out_specs = (P(FSDP, None), P(), P())
    return jax.shard_map(
        shards,
        mesh=split,
        in_specs=in_specs,
        out_specs=out_specs,
        check_vma=False,
    )
```

```python
import math

import jax
import jax.numpy as jnp
from jax import lax
from jax.experimental import pallas as pl
from jax.sharding import Mesh
from jax.sharding import PartitionSpec as P

FSDP = ("fsdp_0", "fsdp_1", "fsdp_2", "fsdp_3")
GROUP_FSDP = ("group", "fsdp_0", "fsdp_1", "fsdp_2", "fsdp_3")
SIZES = (4, 8, 4, 2)
Y, X = 0, 2


epsilon = 1e-06
LARGEST_INPUT = 24.0

RING_ORDER = (0, -1, 1, 2)


def flat(y, z, x, c):
    return ((y * SIZES[1] + z) * SIZES[2] + x) * SIZES[3] + c


def shift_pairs(dims, step):
    pairs = []
    for y in range(SIZES[0]):
        for z in range(SIZES[1]):
            for x in range(SIZES[2]):
                for c in range(SIZES[3]):
                    to = [y, z, x, c]
                    to[dims[c]] = (to[dims[c]] + step) % SIZES[dims[c]]
                    pairs.append((flat(y, z, x, c), flat(*to)))
    return pairs


def shift(value, dims, step):
    return lax.ppermute(value, GROUP_FSDP, shift_pairs(dims, step))


def swap_cores(value):
    return lax.ppermute(value, "fsdp_3", ((0, 1), (1, 0)))


def join_kernel(*refs):
    out = refs[-1]
    at = 0
    for ref in refs[:-1]:
        size = ref.shape[0]
        out[at : at + size, :] = ref[...]
        at += size


def join(parts):
    rows = sum(p.shape[0] for p in parts)
    return pl.pallas_call(
        join_kernel,
        out_shape=jax.ShapeDtypeStruct((rows, parts[0].shape[1]), parts[0].dtype),
        name="join",
    )(*parts)


def ring_gather(block, dims):
    left, right = shift(block, dims, 1), shift(block, dims, -1)
    return block, left, right, shift(left, dims, 1)


def wide_gather(first, second, dims):
    l1, r1 = shift(first, dims, 1), shift(first, dims, -1)
    l2, r2 = shift(second, dims, 1), shift(second, dims, -1)
    far = shift(l1, dims, 1), shift(r2, dims, -1)
    return (first, second), (l1, l2), (r1, r2), far


def power_for(largest):
    return jnp.floor(14.0 - jnp.log2(jnp.maximum(largest, 1e-30)))


def one_hot_rows(index, width, dtype):
    return (index[:, None] == lax.broadcasted_iota(jnp.int32, (1, width), 1)).astype(dtype)


def transposed_dot(left, right):
    return lax.dot_general(
        left, right, (((1,), (1,)), ((), ())), preferred_element_type=jnp.float32
    )


def shards(
    teacher_rows,
    student_rows,
    counts,
    teacher_weight,
    teacher_bias,
    teacher_gain,
    teacher_head,
    cross_weight,
    cross_bias,
    out_weight,
):
    rows = teacher_rows.shape[0]
    width_t = teacher_bias.shape[0]
    width_s = cross_weight.shape[0]
    half_s = width_s // 2
    local = teacher_weight.shape[1]
    loss_scale = math.sqrt(width_s / (rows * lax.axis_size(GROUP_FSDP)))
    y_at = lax.axis_index(("group", "fsdp_0"))
    x_at, core = lax.axis_index("fsdp_2"), lax.axis_index("fsdp_3")
    group = lax.axis_index("group")

    mine = teacher_weight.T
    line = lax.all_to_all(
        jnp.broadcast_to(mine[None], (8, *mine.shape)), "fsdp_1", 0, 0, tiled=True
    ).reshape(8 * local, -1)

    t_rows = jnp.concatenate([teacher_rows, swap_cores(teacher_rows)], axis=0)
    s_rows = jnp.concatenate([student_rows, swap_cores(student_rows)], axis=0)

    vectors = jnp.stack([teacher_bias, teacher_gain, teacher_head]).reshape(3, 4, 8 * 4 * 2 * local)
    order_y = (y_at + jnp.array(RING_ORDER, jnp.int32)) % 4
    order_x = (x_at + jnp.array(RING_ORDER, jnp.int32)) % 4
    units = (
        order_x[:, None, None] * (2 * local)
        + jnp.arange(8, dtype=jnp.int32)[None, :, None] * (8 * local)
        + core * local
        + jnp.arange(local, dtype=jnp.int32)[None, None, :]
    ).reshape(-1)
    exact = lax.Precision.HIGHEST
    vectors = jnp.einsum(
        "wy,vyk->vwk", one_hot_rows(order_y, 4, jnp.float32), vectors, precision=exact
    )
    vectors = lax.dot_general(
        vectors.reshape(12, -1),
        one_hot_rows(units, vectors.shape[2], jnp.float32),
        (((1,), (1,)), ((), ())),
        precision=exact,
    ).reshape(3, 4, 4, 8 * local)
    vectors = jnp.where(core == 0, vectors, vectors.transpose(0, 2, 1, 3))
    vectors = vectors.reshape(3, 4, 2, 16 * local)
    line, vectors, t_rows, s_rows = lax.optimization_barrier((line, vectors, t_rows, s_rows))

    near, wide = (X, Y), (Y, X)
    around = ring_gather(line, near)
    plane = join(around[:2]), join(around[2:])

    cut = core * half_s
    cross_half = lax.dynamic_slice_in_dim(cross_weight, cut, half_s, axis=1)
    cross_bias_half = lax.dynamic_slice_in_dim(cross_bias, cut, half_s)
    out_half = lax.dynamic_slice_in_dim(out_weight, cut, half_s)
    cross = lax.dot_general(
        cross_half, s_rows, (((0,), (1,)), ((), ())), preferred_element_type=jnp.float32
    ) + cross_bias_half[:, None]
    inputs = transposed_dot(
        one_hot_rows(cut + jnp.arange(half_s, dtype=jnp.int32), width_s, s_rows.dtype), s_rows
    )
    mixed = inputs * cross + inputs
    student_part = jnp.sum(mixed * out_half[:, None], axis=0)

    features = (
        jnp.arange(2, dtype=jnp.int32)[:, None, None, None, None] * 8
        + jnp.arange(2, dtype=jnp.int32)[:, None, None, None] * (8 * 4 * 16)
        + jnp.arange(4, dtype=jnp.int32)[:, None, None] * 16
        + jnp.arange(8, dtype=jnp.int32)[:, None] * (4 * 16)
        + jnp.arange(8, dtype=jnp.int32)
    ).reshape(-1)
    turned = transposed_dot(one_hot_rows(features, width_s, s_rows.dtype), s_rows).astype(
        s_rows.dtype
    )
    blocks = wide_gather(*plane, wide)
    last, inputs, mixed, student_part, turned = lax.optimization_barrier(
        (blocks[3][1], inputs, mixed, student_part, turned)
    )
    blocks = (*blocks[:3], (blocks[3][0], last))

    pieces = [(i, j) for i in range(4) for j in range(2)]
    preact, squares = {}, 0.0
    for i, j in pieces:
        p = transposed_dot(blocks[i][j], t_rows) + vectors[0, i, j][:, None]
        preact[i, j] = p
        squares = squares + jnp.sum(p * p, axis=0)

    amount = counts.astype(jnp.float32)
    other = swap_cores(jnp.concatenate([squares, jnp.broadcast_to(amount, (128,))]))
    squares = squares + jnp.concatenate([other[rows : 2 * rows], other[:rows]])
    amounts = jnp.concatenate(
        [jnp.broadcast_to(amount, (rows,)), jnp.broadcast_to(other[2 * rows], (rows,))]
    )

    scale = lax.rsqrt(squares / width_t + epsilon)[None, :]
    logit = 0.0
    for i, j in pieces:
        gain, head = vectors[1, i, j][:, None], vectors[2, i, j][:, None]
        normed = preact[i, j] * scale * gain
        gated = 0.5 * normed * (1.0 + jnp.tanh(0.5 * normed))
        logit = logit + jnp.sum(gated * head, axis=0)
    part = student_part - logit
    other = swap_cores(part)
    differ = part + jnp.concatenate([other[rows:], other[:rows]])
    place = (jnp.arange(2 * rows, dtype=jnp.int32) % rows).astype(jnp.float32)
    error = (differ * (place < amounts).astype(jnp.float32) * loss_scale)[None, :]
    dcross = error * out_half[:, None] * inputs
    dcross_half = dcross.astype(jnp.bfloat16)
    small = jnp.stack([jnp.sum(dcross, axis=1), jnp.sum(error * mixed, axis=1)])

    reach = jnp.max(jnp.sum(jnp.abs(dcross), axis=1)) * LARGEST_INPUT
    power, power_small = power_for(reach), power_for(jnp.max(jnp.abs(small)))
    parts = transposed_dot(turned, dcross_half)
    scaled = small * jnp.exp2(power_small)
    top = scaled.astype(jnp.float16)
    low = (scaled - top.astype(jnp.float32)).astype(jnp.float16)
    powers = jnp.stack([power, power_small]).astype(jnp.float16)
    tail = jnp.concatenate(
        [top, low, jnp.broadcast_to(powers[:, None], (2, half_s)), jnp.zeros_like(top)], axis=0
    )
    parts = (parts * jnp.exp2(power)).astype(jnp.float16).reshape(16, -1, half_s)
    parts = jnp.concatenate([parts, jnp.broadcast_to(tail, (16, *tail.shape))], axis=1)
    parts = lax.all_to_all(parts, ("group", "fsdp_0", "fsdp_2"), 0, 0, tiled=True)
    tail = parts[:, -8:].astype(jnp.float32)
    small = ((tail[:, :2] + tail[:, 2:4]) * jnp.exp2(-tail[:, 5:6])).sum(axis=0)
    parts = parts[:, :-8].astype(jnp.float32) * jnp.exp2(-tail[:, 4:5, :1])
    parts = parts.sum(axis=0).reshape(8, 8, half_s)
    small = small.reshape(8, half_s // 4)
    parts = jnp.concatenate(
        [parts, jnp.broadcast_to(small, (8, *small.shape))], axis=2
    )
    parts = lax.all_to_all(parts, "fsdp_1", 0, 0, tiled=True).sum(axis=0)
    got = [
        lax.ppermute(parts, ("group", "fsdp_3"), pairs)
        for pairs in (((0, 0), (1, 2), (2, 1), (3, 3)), ((0, 2), (1, 0), (2, 3), (3, 1)))
    ]
    low = jnp.where(group == 0, got[0], got[1])
    high = jnp.where(group == 0, got[1], got[0])
    grad_cross = jnp.concatenate([low[:, :half_s], high[:, :half_s]], axis=1)
    small = jnp.concatenate(
        [low[:, half_s:].reshape(2, half_s), high[:, half_s:].reshape(2, half_s)], axis=1
    )
    return grad_cross, small[0], small[1]


def solution(mesh):
    split = Mesh(mesh.devices.reshape(2, 2, 8, 4, 2), GROUP_FSDP)
    in_specs = (
        P(GROUP_FSDP, None),
        P(GROUP_FSDP, None),
        P(GROUP_FSDP),
        P(None, GROUP_FSDP),
        P(),
        P(),
        P(),
        P(),
        P(),
        P(),
    )
    out_specs = (P(FSDP, None), P(), P())
    return jax.shard_map(
        shards,
        mesh=split,
        in_specs=in_specs,
        out_specs=out_specs,
        check_vma=False,
    )
```

```python
import math

import jax
import jax.numpy as jnp
from jax import lax
from jax.experimental import pallas as pl
from jax.experimental.pallas import tpu as pltpu
from jax.sharding import Mesh
from jax.sharding import PartitionSpec as P

FSDP = ("fsdp_0", "fsdp_1", "fsdp_2", "fsdp_3")
GROUP_FSDP = ("group", "fsdp_0", "fsdp_1", "fsdp_2", "fsdp_3")
SIZES = (4, 8, 4, 2)
Y, X = 0, 2


epsilon = 1e-06
LARGEST_INPUT = 24.0

RING_ORDER = (0, -1, 1, 2)


def flat(y, z, x, c):
    return ((y * SIZES[1] + z) * SIZES[2] + x) * SIZES[3] + c


def shift_pairs(dims, step):
    pairs = []
    for y in range(SIZES[0]):
        for z in range(SIZES[1]):
            for x in range(SIZES[2]):
                for c in range(SIZES[3]):
                    to = [y, z, x, c]
                    to[dims[c]] = (to[dims[c]] + step) % SIZES[dims[c]]
                    pairs.append((flat(y, z, x, c), flat(*to)))
    return pairs


def shift(value, dims, step):
    return lax.ppermute(value, GROUP_FSDP, shift_pairs(dims, step))


def swap_cores(value):
    return lax.ppermute(value, "fsdp_3", ((0, 1), (1, 0)))


def join_kernel(*refs):
    out = refs[-1]
    at = 0
    for ref in refs[:-1]:
        size = ref.shape[0]
        out[at : at + size, :] = ref[...]
        at += size


def join(parts):
    rows = sum(p.shape[0] for p in parts)
    return pl.pallas_call(
        join_kernel,
        out_shape=jax.ShapeDtypeStruct((rows, parts[0].shape[1]), parts[0].dtype),
        compiler_params=pltpu.CompilerParams(vmem_limit_bytes=4 * 2**20),
        name="join",
    )(*parts)


def ring_gather(block, dims):
    left, right = shift(block, dims, 1), shift(block, dims, -1)
    return block, left, right, shift(left, dims, 1)


def wide_gather(first, second, dims):
    l1, r1 = shift(first, dims, 1), shift(first, dims, -1)
    l2, r2 = shift(second, dims, 1), shift(second, dims, -1)
    far = shift(l1, dims, 1), shift(r2, dims, -1)
    return (first, second), (l1, l2), (r1, r2), far


def power_for(largest):
    return jnp.floor(14.0 - jnp.log2(jnp.maximum(largest, 1e-30)))


def one_hot_rows(index, width, dtype):
    return (index[:, None] == lax.broadcasted_iota(jnp.int32, (1, width), 1)).astype(dtype)


def transposed_dot(left, right):
    return lax.dot_general(
        left, right, (((1,), (1,)), ((), ())), preferred_element_type=jnp.float32
    )


def shards(
    teacher_rows,
    student_rows,
    counts,
    teacher_weight,
    teacher_bias,
    teacher_gain,
    teacher_head,
    cross_weight,
    cross_bias,
    out_weight,
):
    rows = teacher_rows.shape[0]
    width_t = teacher_bias.shape[0]
    width_s = cross_weight.shape[0]
    half_s = width_s // 2
    local = teacher_weight.shape[1]
    loss_scale = math.sqrt(width_s / (rows * lax.axis_size(GROUP_FSDP)))
    y_at = lax.axis_index(("group", "fsdp_0"))
    x_at, core = lax.axis_index("fsdp_2"), lax.axis_index("fsdp_3")
    group = lax.axis_index("group")

    mine = teacher_weight.T
    line = lax.all_to_all(
        jnp.broadcast_to(mine[None], (8, *mine.shape)), "fsdp_1", 0, 0, tiled=True
    ).reshape(8 * local, -1)

    t_rows = jnp.concatenate([teacher_rows, swap_cores(teacher_rows)], axis=0)
    s_rows = jnp.concatenate([student_rows, swap_cores(student_rows)], axis=0)

    vectors = jnp.stack([teacher_bias, teacher_gain, teacher_head]).reshape(3, 4, 8 * 4 * 2 * local)
    order_y = (y_at + jnp.array(RING_ORDER, jnp.int32)) % 4
    order_x = (x_at + jnp.array(RING_ORDER, jnp.int32)) % 4
    units = (
        order_x[:, None, None] * (2 * local)
        + jnp.arange(8, dtype=jnp.int32)[None, :, None] * (8 * local)
        + core * local
        + jnp.arange(local, dtype=jnp.int32)[None, None, :]
    ).reshape(-1)
    exact = lax.Precision.HIGHEST
    vectors = jnp.einsum(
        "wy,vyk->vwk", one_hot_rows(order_y, 4, jnp.float32), vectors, precision=exact
    )
    vectors = lax.dot_general(
        vectors.reshape(12, -1),
        one_hot_rows(units, vectors.shape[2], jnp.float32),
        (((1,), (1,)), ((), ())),
        precision=exact,
    ).reshape(3, 4, 4, 8 * local)
    vectors = jnp.where(core == 0, vectors, vectors.transpose(0, 2, 1, 3))
    vectors = vectors.reshape(3, 4, 2, 16 * local)
    line, vectors, t_rows, s_rows = lax.optimization_barrier((line, vectors, t_rows, s_rows))

    near, wide = (X, Y), (Y, X)
    around = ring_gather(line, near)
    plane = join(around[:2]), join(around[2:])

    cut = core * half_s
    cross_half = lax.dynamic_slice_in_dim(cross_weight, cut, half_s, axis=1)
    cross_bias_half = lax.dynamic_slice_in_dim(cross_bias, cut, half_s)
    out_half = lax.dynamic_slice_in_dim(out_weight, cut, half_s)
    cross = lax.dot_general(
        cross_half, s_rows, (((0,), (1,)), ((), ())), preferred_element_type=jnp.float32
    ) + cross_bias_half[:, None]
    inputs = transposed_dot(
        one_hot_rows(cut + jnp.arange(half_s, dtype=jnp.int32), width_s, s_rows.dtype), s_rows
    ).astype(s_rows.dtype)
    mixed = inputs.astype(jnp.float32) * cross + inputs.astype(jnp.float32)
    student_part = jnp.sum(mixed * out_half[:, None], axis=0)

    features = (
        jnp.arange(2, dtype=jnp.int32)[:, None, None, None, None] * 8
        + jnp.arange(2, dtype=jnp.int32)[:, None, None, None] * (8 * 4 * 16)
        + jnp.arange(4, dtype=jnp.int32)[:, None, None] * 16
        + jnp.arange(8, dtype=jnp.int32)[:, None] * (4 * 16)
        + jnp.arange(8, dtype=jnp.int32)
    ).reshape(-1)
    turned = transposed_dot(one_hot_rows(features, width_s, s_rows.dtype), s_rows).astype(
        s_rows.dtype
    )
    blocks = wide_gather(*plane, wide)
    last, inputs, mixed, student_part, turned = lax.optimization_barrier(
        (blocks[3][1], inputs, mixed, student_part, turned)
    )
    blocks = (*blocks[:3], (blocks[3][0], last))

    pieces = [(i, j) for i in range(4) for j in range(2)]
    preact, squares = {}, 0.0
    for i, j in pieces:
        p = transposed_dot(blocks[i][j], t_rows) + vectors[0, i, j][:, None]
        preact[i, j] = p
        squares = squares + jnp.sum(p * p, axis=0)

    amount = counts.astype(jnp.float32)
    other = swap_cores(jnp.concatenate([squares, jnp.broadcast_to(amount, (128,))]))
    squares = squares + jnp.concatenate([other[rows : 2 * rows], other[:rows]])
    amounts = jnp.concatenate(
        [jnp.broadcast_to(amount, (rows,)), jnp.broadcast_to(other[2 * rows], (rows,))]
    )

    scale = lax.rsqrt(squares / width_t + epsilon)[None, :]
    logit = 0.0
    for i, j in pieces:
        gain, head = vectors[1, i, j][:, None], vectors[2, i, j][:, None]
        normed = preact[i, j] * scale * gain
        gated = 0.5 * normed * (1.0 + jnp.tanh(0.5 * normed))
        logit = logit + jnp.sum(gated * head, axis=0)
    part = student_part - logit
    other = swap_cores(part)
    differ = part + jnp.concatenate([other[rows:], other[:rows]])
    place = (jnp.arange(2 * rows, dtype=jnp.int32) % rows).astype(jnp.float32)
    error = (differ * (place < amounts).astype(jnp.float32) * loss_scale)[None, :]
    dcross = error * out_half[:, None] * inputs.astype(jnp.float32)
    dcross_half = dcross.astype(jnp.bfloat16)
    small = jnp.stack([jnp.sum(dcross, axis=1), jnp.sum(error * mixed, axis=1)])
    reach = jnp.maximum(jnp.sum(jnp.abs(dcross), axis=1) * LARGEST_INPUT, jnp.abs(small[1]))

    dcross_half, reach, small = lax.optimization_barrier((dcross_half, reach, small))
    parts = transposed_dot(turned, dcross_half)
    power = power_for(jnp.max(reach))
    scaled = small * jnp.exp2(power)
    top = scaled.astype(jnp.float16)
    low = (scaled - top.astype(jnp.float32)).astype(jnp.float16)
    powers = jnp.broadcast_to(power.astype(jnp.float16), (4, half_s))
    tail = jnp.concatenate([top, low, powers], axis=0)
    parts = (parts * jnp.exp2(power)).astype(jnp.float16).reshape(16, -1, half_s)
    parts = jnp.concatenate([parts, jnp.broadcast_to(tail, (16, *tail.shape))], axis=1)
    parts = lax.all_to_all(parts, ("group", "fsdp_0", "fsdp_2"), 0, 0, tiled=True)
    tail = parts[:, -8:].astype(jnp.float32)
    scale = jnp.exp2(-tail[:, 4:5, :1])
    small = ((tail[:, :2] + tail[:, 2:4]) * scale).sum(axis=0)
    parts = (parts[:, :-8].astype(jnp.float32) * scale).sum(axis=0).reshape(8, 8, half_s)
    small = small.reshape(8, half_s // 4)
    parts = jnp.concatenate(
        [parts, jnp.broadcast_to(small, (8, *small.shape))], axis=2
    )
    parts = lax.all_to_all(parts, "fsdp_1", 0, 0, tiled=True).sum(axis=0)
    got = [
        lax.ppermute(parts, ("group", "fsdp_3"), pairs)
        for pairs in (((0, 0), (1, 2), (2, 1), (3, 3)), ((0, 2), (1, 0), (2, 3), (3, 1)))
    ]
    low = jnp.where(group == 0, got[0], got[1])
    high = jnp.where(group == 0, got[1], got[0])
    grad_cross = jnp.concatenate([low[:, :half_s], high[:, :half_s]], axis=1)
    small = jnp.concatenate(
        [low[:, half_s:].reshape(2, half_s), high[:, half_s:].reshape(2, half_s)], axis=1
    )
    return grad_cross, small[0], small[1]


def solution(mesh):
    split = Mesh(mesh.devices.reshape(2, 2, 8, 4, 2), GROUP_FSDP)
    in_specs = (
        P(GROUP_FSDP, None),
        P(GROUP_FSDP, None),
        P(GROUP_FSDP),
        P(None, GROUP_FSDP),
        P(),
        P(),
        P(),
        P(),
        P(),
        P(),
    )
    out_specs = (P(FSDP, None), P(), P())
    return jax.shard_map(
        shards,
        mesh=split,
        in_specs=in_specs,
        out_specs=out_specs,
        check_vma=False,
    )
```

```python
import math

import jax
import jax.numpy as jnp
from jax import lax
from jax.experimental import pallas as pl
from jax.experimental.pallas import tpu as pltpu
from jax.sharding import Mesh
from jax.sharding import PartitionSpec as P

FSDP = ("fsdp_0", "fsdp_1", "fsdp_2", "fsdp_3")
GROUP_FSDP = ("group", "fsdp_0", "fsdp_1", "fsdp_2", "fsdp_3")
SIZES = (4, 8, 4, 2)
Y, X = 0, 2


epsilon = 1e-06
LARGEST_INPUT = 24.0

RING_ORDER = (0, -1, 1, 2)


def flat(y, z, x, c):
    return ((y * SIZES[1] + z) * SIZES[2] + x) * SIZES[3] + c


def shift_pairs(dims, step):
    pairs = []
    for y in range(SIZES[0]):
        for z in range(SIZES[1]):
            for x in range(SIZES[2]):
                for c in range(SIZES[3]):
                    to = [y, z, x, c]
                    to[dims[c]] = (to[dims[c]] + step) % SIZES[dims[c]]
                    pairs.append((flat(y, z, x, c), flat(*to)))
    return pairs


def shift(value, dims, step):
    return lax.ppermute(value, GROUP_FSDP, shift_pairs(dims, step))


def swap_cores(value):
    return lax.ppermute(value, "fsdp_3", ((0, 1), (1, 0)))


def join_kernel(*refs):
    out = refs[-1]
    at = 0
    for ref in refs[:-1]:
        size = ref.shape[0]
        out[at : at + size, :] = ref[...]
        at += size


def join(parts):
    rows = sum(p.shape[0] for p in parts)
    return pl.pallas_call(
        join_kernel,
        out_shape=jax.ShapeDtypeStruct((rows, parts[0].shape[1]), parts[0].dtype),
        compiler_params=pltpu.CompilerParams(vmem_limit_bytes=4 * 2**20),
        name="join",
    )(*parts)


def ring_gather(block, dims):
    half = block.shape[0] // 2
    left, right = shift(block, dims, 1), shift(block, dims, -1)
    far = shift(left[:half], dims, 1), shift(right[half:], dims, -1)
    return block, left, right, *far


def wide_gather(first, second, dims):
    l1, r1 = shift(first, dims, 1), shift(first, dims, -1)
    l2, r2 = shift(second, dims, 1), shift(second, dims, -1)
    far = shift(l1, dims, 1), shift(r2, dims, -1)
    return (first, second), (l1, l2), (r1, r2), far


def power_for(largest):
    return jnp.floor(14.0 - jnp.log2(jnp.maximum(largest, 1e-30)))


def one_hot_rows(index, width, dtype):
    return (index[:, None] == lax.broadcasted_iota(jnp.int32, (1, width), 1)).astype(dtype)


def transposed_dot(left, right):
    return lax.dot_general(
        left, right, (((1,), (1,)), ((), ())), preferred_element_type=jnp.float32
    )


def shards(
    teacher_rows,
    student_rows,
    counts,
    teacher_weight,
    teacher_bias,
    teacher_gain,
    teacher_head,
    cross_weight,
    cross_bias,
    out_weight,
):
    rows = teacher_rows.shape[0]
    width_t = teacher_bias.shape[0]
    width_s = cross_weight.shape[0]
    half_s = width_s // 2
    local = teacher_weight.shape[1]
    loss_scale = math.sqrt(width_s / (rows * lax.axis_size(GROUP_FSDP)))
    y_at = lax.axis_index(("group", "fsdp_0"))
    x_at, core = lax.axis_index("fsdp_2"), lax.axis_index("fsdp_3")
    group = lax.axis_index("group")

    mine = teacher_weight.T
    line = lax.all_to_all(
        jnp.broadcast_to(mine[None], (8, *mine.shape)), "fsdp_1", 0, 0, tiled=True
    ).reshape(8 * local, -1)

    t_rows = jnp.concatenate([teacher_rows, swap_cores(teacher_rows)], axis=0)
    s_rows = jnp.concatenate([student_rows, swap_cores(student_rows)], axis=0)

    vectors = jnp.stack([teacher_bias, teacher_gain, teacher_head]).reshape(3, 4, 8 * 4 * 2 * local)
    order_y = (y_at + jnp.array(RING_ORDER, jnp.int32)) % 4
    order_x = (x_at + jnp.array(RING_ORDER, jnp.int32)) % 4
    units = (
        order_x[:, None, None] * (2 * local)
        + jnp.arange(8, dtype=jnp.int32)[None, :, None] * (8 * local)
        + core * local
        + jnp.arange(local, dtype=jnp.int32)[None, None, :]
    ).reshape(-1)
    exact = lax.Precision.HIGHEST
    vectors = jnp.einsum(
        "wy,vyk->vwk", one_hot_rows(order_y, 4, jnp.float32), vectors, precision=exact
    )
    vectors = lax.dot_general(
        vectors.reshape(12, -1),
        one_hot_rows(units, vectors.shape[2], jnp.float32),
        (((1,), (1,)), ((), ())),
        precision=exact,
    ).reshape(3, 4, 4, 8 * local)
    vectors = jnp.where(core == 0, vectors, vectors.transpose(0, 2, 1, 3))
    vectors = vectors.reshape(3, 4, 2, 16 * local)
    line, vectors, t_rows, s_rows = lax.optimization_barrier((line, vectors, t_rows, s_rows))

    near, wide = (X, Y), (Y, X)
    around = ring_gather(line, near)
    plane = join(around[:2]), join(around[2:])

    cut = core * half_s
    cross_half = lax.dynamic_slice_in_dim(cross_weight, cut, half_s, axis=1)
    cross_bias_half = lax.dynamic_slice_in_dim(cross_bias, cut, half_s)
    out_half = lax.dynamic_slice_in_dim(out_weight, cut, half_s)
    cross = lax.dot_general(
        cross_half, s_rows, (((0,), (1,)), ((), ())), preferred_element_type=jnp.float32
    ) + cross_bias_half[:, None]
    flipped = lax.optimization_barrier(s_rows.T)
    inputs = lax.dynamic_slice_in_dim(flipped, cut, half_s, axis=0)
    mixed = inputs.astype(jnp.float32) * cross + inputs.astype(jnp.float32)
    student_part = jnp.sum(mixed * out_half[:, None], axis=0)

    turned = flipped.reshape(2, 8, 4, 2, 8, -1).transpose(3, 0, 2, 1, 4, 5)
    turned = turned.reshape(flipped.shape)
    blocks = wide_gather(*plane, wide)
    last, inputs, mixed, student_part, turned = lax.optimization_barrier(
        (blocks[3][1], inputs, mixed, student_part, turned)
    )
    blocks = (*blocks[:3], (blocks[3][0], last))

    pieces = [(i, j) for i in range(4) for j in range(2)]
    preact, squares = {}, 0.0
    for i, j in pieces:
        p = transposed_dot(blocks[i][j], t_rows) + vectors[0, i, j][:, None]
        preact[i, j] = p
        squares = squares + jnp.sum(p * p, axis=0)

    amount = counts.astype(jnp.float32)
    other = swap_cores(jnp.concatenate([squares, jnp.broadcast_to(amount, (128,))]))
    squares = squares + jnp.concatenate([other[rows : 2 * rows], other[:rows]])
    amounts = jnp.concatenate(
        [jnp.broadcast_to(amount, (rows,)), jnp.broadcast_to(other[2 * rows], (rows,))]
    )

    scale = lax.rsqrt(squares / width_t + epsilon)[None, :]
    logit = 0.0
    for i, j in pieces:
        gain, head = vectors[1, i, j][:, None], vectors[2, i, j][:, None]
        normed = preact[i, j] * scale * gain
        gated = 0.5 * normed * (1.0 + jnp.tanh(0.5 * normed))
        logit = logit + jnp.sum(gated * head, axis=0)
    part = student_part - logit
    other = swap_cores(part)
    differ = part + jnp.concatenate([other[rows:], other[:rows]])
    place = (jnp.arange(2 * rows, dtype=jnp.int32) % rows).astype(jnp.float32)
    error = (differ * (place < amounts).astype(jnp.float32) * loss_scale)[None, :]
    dcross = error * out_half[:, None] * inputs.astype(jnp.float32)
    dcross_half = dcross.astype(jnp.bfloat16)
    small = jnp.stack([jnp.sum(dcross, axis=1), jnp.sum(error * mixed, axis=1)])
    reach = jnp.maximum(jnp.sum(jnp.abs(dcross), axis=1) * LARGEST_INPUT, jnp.abs(small[1]))

    dcross_half, reach, small = lax.optimization_barrier((dcross_half, reach, small))
    parts = transposed_dot(turned, dcross_half)
    power = power_for(jnp.max(reach, keepdims=True))[:, None]
    scaled = small * jnp.exp2(power)
    top = scaled.astype(jnp.float16)
    low = (scaled - top.astype(jnp.float32)).astype(jnp.float16)
    powers = jnp.broadcast_to(power, (4, half_s)).astype(jnp.float16)
    tail = jnp.concatenate([top, low, powers], axis=0)
    parts = (parts * jnp.exp2(power)).astype(jnp.float16).reshape(16, -1, half_s)
    parts = jnp.concatenate([parts, jnp.broadcast_to(tail, (16, *tail.shape))], axis=1)
    parts = lax.all_to_all(parts, ("group", "fsdp_0", "fsdp_2"), 0, 0, tiled=True)
    tail = parts[:, -8:].astype(jnp.float32)
    scale = jnp.exp2(-tail[:, 4:5, :1])
    small = ((tail[:, :2] + tail[:, 2:4]) * scale).sum(axis=0)
    parts = (parts[:, :-8].astype(jnp.float32) * scale).sum(axis=0).reshape(8, 8, half_s)
    small = small.reshape(8, half_s // 4)
    parts = jnp.concatenate(
        [parts, jnp.broadcast_to(small, (8, *small.shape))], axis=2
    )
    parts = lax.all_to_all(parts, "fsdp_1", 0, 0, tiled=True).sum(axis=0)
    got = [
        lax.ppermute(parts, ("group", "fsdp_3"), pairs)
        for pairs in (((0, 0), (1, 2), (2, 1), (3, 3)), ((0, 2), (1, 0), (2, 3), (3, 1)))
    ]
    low = jnp.where(group == 0, got[0], got[1])
    high = jnp.where(group == 0, got[1], got[0])
    grad_cross = jnp.concatenate([low[:, :half_s], high[:, :half_s]], axis=1)
    small = jnp.concatenate(
        [low[:, half_s:].reshape(2, half_s), high[:, half_s:].reshape(2, half_s)], axis=1
    )
    return grad_cross, small[0], small[1]


def solution(mesh):
    split = Mesh(mesh.devices.reshape(2, 2, 8, 4, 2), GROUP_FSDP)
    in_specs = (
        P(GROUP_FSDP, None),
        P(GROUP_FSDP, None),
        P(GROUP_FSDP),
        P(None, GROUP_FSDP),
        P(),
        P(),
        P(),
        P(),
        P(),
        P(),
    )
    out_specs = (P(FSDP, None), P(), P())
    return jax.shard_map(
        shards,
        mesh=split,
        in_specs=in_specs,
        out_specs=out_specs,
        check_vma=False,
    )
```

```python
import math

import jax
import jax.numpy as jnp
from jax import lax
from jax.experimental import pallas as pl
from jax.experimental.pallas import tpu as pltpu
from jax.sharding import Mesh
from jax.sharding import PartitionSpec as P

FSDP = ("fsdp_0", "fsdp_1", "fsdp_2", "fsdp_3")
GROUP_FSDP = ("group", "fsdp_0", "fsdp_1", "fsdp_2", "fsdp_3")
SIZES = (4, 8, 4, 2)
Y, X = 0, 2


epsilon = 1e-06
LARGEST_INPUT = 24.0

RING_ORDER = (0, -1, 1, 2)


def flat(y, z, x, c):
    return ((y * SIZES[1] + z) * SIZES[2] + x) * SIZES[3] + c


def shift_pairs(dims, step):
    pairs = []
    for y in range(SIZES[0]):
        for z in range(SIZES[1]):
            for x in range(SIZES[2]):
                for c in range(SIZES[3]):
                    to = [y, z, x, c]
                    to[dims[c]] = (to[dims[c]] + step) % SIZES[dims[c]]
                    pairs.append((flat(y, z, x, c), flat(*to)))
    return pairs


def shift(value, dims, step):
    return lax.ppermute(value, GROUP_FSDP, shift_pairs(dims, step))


def swap_cores(value):
    return lax.ppermute(value, "fsdp_3", ((0, 1), (1, 0)))


def join_kernel(*refs):
    out = refs[-1]
    at = 0
    for ref in refs[:-1]:
        size = ref.shape[0]
        out[at : at + size, :] = ref[...]
        at += size


def join(parts):
    rows = sum(p.shape[0] for p in parts)
    return pl.pallas_call(
        join_kernel,
        out_shape=jax.ShapeDtypeStruct((rows, parts[0].shape[1]), parts[0].dtype),
        compiler_params=pltpu.CompilerParams(vmem_limit_bytes=4 * 2**20),
        name="join",
    )(*parts)


def ring_gather(block, dims):
    left, right = shift(block, dims, 1), shift(block, dims, -1)
    return block, left, right, shift(left, dims, 1)


def wide_gather(first, second, dims):
    l1, r1 = shift(first, dims, 1), shift(first, dims, -1)
    l2, r2 = shift(second, dims, 1), shift(second, dims, -1)
    far = shift(l1, dims, 1), shift(r2, dims, -1)
    return (first, second), (l1, l2), (r1, r2), far


def power_for(largest):
    return jnp.floor(14.0 - jnp.log2(jnp.maximum(largest, 1e-30)))


def one_hot_rows(index, width, dtype):
    return (index[:, None] == lax.broadcasted_iota(jnp.int32, (1, width), 1)).astype(dtype)


def transposed_dot(left, right):
    return lax.dot_general(
        left, right, (((1,), (1,)), ((), ())), preferred_element_type=jnp.float32
    )


def shards(
    teacher_rows,
    student_rows,
    counts,
    teacher_weight,
    teacher_bias,
    teacher_gain,
    teacher_head,
    cross_weight,
    cross_bias,
    out_weight,
):
    rows = teacher_rows.shape[0]
    width_t = teacher_bias.shape[0]
    width_s = cross_weight.shape[0]
    half_s = width_s // 2
    local = teacher_weight.shape[1]
    loss_scale = math.sqrt(width_s / (rows * lax.axis_size(GROUP_FSDP)))
    y_at = lax.axis_index(("group", "fsdp_0"))
    x_at, core = lax.axis_index("fsdp_2"), lax.axis_index("fsdp_3")
    group = lax.axis_index("group")

    mine = teacher_weight.T
    line = lax.all_to_all(
        jnp.broadcast_to(mine[None], (8, *mine.shape)), "fsdp_1", 0, 0, tiled=True
    ).reshape(8 * local, -1)

    t_rows = jnp.concatenate([teacher_rows, swap_cores(teacher_rows)], axis=0)
    s_rows = jnp.concatenate([student_rows, swap_cores(student_rows)], axis=0)

    vectors = jnp.stack([teacher_bias, teacher_gain, teacher_head]).reshape(3, 4, 8 * 4 * 2 * local)
    order_y = (y_at + jnp.array(RING_ORDER, jnp.int32)) % 4
    order_x = (x_at + jnp.array(RING_ORDER, jnp.int32)) % 4
    units = (
        order_x[:, None, None] * (2 * local)
        + jnp.arange(8, dtype=jnp.int32)[None, :, None] * (8 * local)
        + core * local
        + jnp.arange(local, dtype=jnp.int32)[None, None, :]
    ).reshape(-1)
    exact = lax.Precision.HIGHEST
    vectors = jnp.einsum(
        "wy,vyk->vwk", one_hot_rows(order_y, 4, jnp.float32), vectors, precision=exact
    )
    vectors = lax.dot_general(
        vectors.reshape(12, -1),
        one_hot_rows(units, vectors.shape[2], jnp.float32),
        (((1,), (1,)), ((), ())),
        precision=exact,
    ).reshape(3, 4, 4, 8 * local)
    vectors = jnp.where(core == 0, vectors, vectors.transpose(0, 2, 1, 3))
    vectors = vectors.reshape(3, 4, 2, 16 * local)
    line, vectors, t_rows, s_rows = lax.optimization_barrier((line, vectors, t_rows, s_rows))

    near, wide = (X, Y), (Y, X)
    around = ring_gather(line, near)
    plane = join(around[:2]), join(around[2:])

    cut = core * half_s
    cross_half = lax.dynamic_slice_in_dim(cross_weight, cut, half_s, axis=1)
    cross_bias_half = lax.dynamic_slice_in_dim(cross_bias, cut, half_s)
    out_half = lax.dynamic_slice_in_dim(out_weight, cut, half_s)
    cross = lax.dot_general(
        cross_half, s_rows, (((0,), (1,)), ((), ())), preferred_element_type=jnp.float32
    ) + cross_bias_half[:, None]
    flipped = lax.optimization_barrier(s_rows.T)
    inputs = lax.dynamic_slice_in_dim(flipped, cut, half_s, axis=0)
    mixed = inputs.astype(jnp.float32) * cross + inputs.astype(jnp.float32)
    student_part = jnp.sum(mixed * out_half[:, None], axis=0)

    turned = flipped.reshape(2, 8, 4, 2, 8, -1).transpose(3, 0, 2, 1, 4, 5)
    turned = turned.reshape(flipped.shape)
    blocks = wide_gather(*plane, wide)
    last, inputs, mixed, student_part, turned = lax.optimization_barrier(
        (blocks[3][1], inputs, mixed, student_part, turned)
    )
    blocks = (*blocks[:3], (blocks[3][0], last))

    pieces = [(i, j) for i in range(4) for j in range(2)]
    preact, squares = {}, 0.0
    for i, j in pieces:
        p = transposed_dot(blocks[i][j], t_rows) + vectors[0, i, j][:, None]
        preact[i, j] = p
        squares = squares + jnp.sum(p * p, axis=0)

    amount = counts.astype(jnp.float32)
    other = swap_cores(jnp.concatenate([squares, jnp.broadcast_to(amount, (128,))]))
    squares = squares + jnp.concatenate([other[rows : 2 * rows], other[:rows]])
    amounts = jnp.concatenate(
        [jnp.broadcast_to(amount, (rows,)), jnp.broadcast_to(other[2 * rows], (rows,))]
    )

    scale = lax.rsqrt(squares / width_t + epsilon)[None, :]
    logit = 0.0
    for i, j in pieces:
        gain, head = vectors[1, i, j][:, None], vectors[2, i, j][:, None]
        normed = preact[i, j] * scale * gain
        gated = 0.5 * normed * (1.0 + jnp.tanh(0.5 * normed))
        logit = logit + jnp.sum(gated * head, axis=0)
    part = student_part - logit
    other = swap_cores(part)
    differ = part + jnp.concatenate([other[rows:], other[:rows]])
    place = (jnp.arange(2 * rows, dtype=jnp.int32) % rows).astype(jnp.float32)
    error = (differ * (place < amounts).astype(jnp.float32) * loss_scale)[None, :]
    dcross = error * out_half[:, None] * inputs.astype(jnp.float32)
    dcross_half = dcross.astype(jnp.bfloat16)
    small = jnp.stack([jnp.sum(dcross, axis=1), jnp.sum(error * mixed, axis=1)])
    reach = jnp.maximum(jnp.sum(jnp.abs(dcross), axis=1) * LARGEST_INPUT, jnp.abs(small[1]))

    dcross_half, reach, small = lax.optimization_barrier((dcross_half, reach, small))
    parts = transposed_dot(turned, dcross_half)
    power = power_for(jnp.max(reach))
    scaled = small * jnp.exp2(power)
    top = scaled.astype(jnp.float16)
    low = (scaled - top.astype(jnp.float32)).astype(jnp.float16)
    powers = jnp.broadcast_to(power.astype(jnp.float16), (4, half_s))
    tail = jnp.concatenate([top, low, powers], axis=0)
    parts = (parts * jnp.exp2(power)).astype(jnp.float16).reshape(16, -1, half_s)
    parts = jnp.concatenate([parts, jnp.broadcast_to(tail, (16, *tail.shape))], axis=1)
    parts = lax.all_to_all(parts, ("group", "fsdp_0", "fsdp_2"), 0, 0, tiled=True)
    tail = parts[:, -8:].astype(jnp.float32)
    scale = jnp.exp2(-tail[:, 4:5, :1])
    small = ((tail[:, :2] + tail[:, 2:4]) * scale).sum(axis=0)
    parts = (parts[:, :-8].astype(jnp.float32) * scale).sum(axis=0).reshape(8, 8, half_s)
    small = small.reshape(8, half_s // 4)
    parts = jnp.concatenate(
        [parts, jnp.broadcast_to(small, (8, *small.shape))], axis=2
    )
    parts = lax.all_to_all(parts, "fsdp_1", 0, 0, tiled=True).sum(axis=0)
    got = [
        lax.ppermute(parts, ("group", "fsdp_3"), pairs)
        for pairs in (((0, 0), (1, 2), (2, 1), (3, 3)), ((0, 2), (1, 0), (2, 3), (3, 1)))
    ]
    low = jnp.where(group == 0, got[0], got[1])
    high = jnp.where(group == 0, got[1], got[0])
    grad_cross = jnp.concatenate([low[:, :half_s], high[:, :half_s]], axis=1)
    small = jnp.concatenate(
        [low[:, half_s:].reshape(2, half_s), high[:, half_s:].reshape(2, half_s)], axis=1
    )
    return grad_cross, small[0], small[1]


def solution(mesh):
    split = Mesh(mesh.devices.reshape(2, 2, 8, 4, 2), GROUP_FSDP)
    in_specs = (
        P(GROUP_FSDP, None),
        P(GROUP_FSDP, None),
        P(GROUP_FSDP),
        P(None, GROUP_FSDP),
        P(),
        P(),
        P(),
        P(),
        P(),
        P(),
    )
    out_specs = (P(FSDP, None), P(), P())
    return jax.shard_map(
        shards,
        mesh=split,
        in_specs=in_specs,
        out_specs=out_specs,
        check_vma=False,
    )
```
